32 devices in a mesh: layer: 4 (over y, x), trace: 8 (over z, core).
Axes of the slice: x: 2, y: 2, z: 4, core: 2. Of those that a mesh axis runs over, the one named last changes fastest.
Arguments:
- operators: bfloat16 [4, 48, 512, 512], P('layer', 'trace'), may hold values from -0.25 to 0.25
- sources: bfloat16 [4, 2, 131072, 128], P('layer', None, 'trace'), may hold values from -6 to 6
- row_block: int32 [4, 8, 6], P('layer'), may hold values from 0 to 255, as said below
- col_block: int32 [4, 8, 6], P('layer', 'trace'), may hold values from 0 to 255, as said below
Outputs:
- traces: bfloat16 [4, 2, 131072, 128], P('layer', None, 'trace')
The draws below stay inside these ranges and needn't reach their ends.
Inputs may be any that keep to these rules, and one draw needn't show every extreme that they name: `row_block`: for each layer and each trace index d, the 6 row blocks name distinct owners; in each layer some owner is named by every d, and so are owners 0 and 7. `col_block`: entries of trace index d lie in d * 32 to (d + 1) * 32 - 1.
All inputs are finite; a program needn't handle non-finite values.
Results may differ from the reference program's by a relative error of at most 0.0077.
Values may be sent and summed in bfloat16 or wider, within the bound.
No kernel may reach another device: no remote copies, remote signals or barrier semaphores. Data moves between devices by JAX's collectives and lax.ppermute only.
A program may use at most 128 MiB of HBM per device.

```python
import jax
import jax.numpy as jnp
from jax import lax

TRACE_ROWS = 131072
BLOCK = 512
SHOTS = 128
BATCHES = 2
N_LAYERS = 4
BLK_DEV = 32
BLOCKS_DEV = 6
N_LAYER = 4
N_TRACE = 8


def pattern(key):
    base = jax.random.fold_in(key, 7)
    hotter = jax.random.randint(jax.random.fold_in(base, 1), (N_LAYER,), 0, N_TRACE)
    keys = jax.random.split(jax.random.fold_in(base, 2), N_LAYER * N_TRACE)
    orders = jax.vmap(lambda sub: jax.random.permutation(sub, N_TRACE))(keys).reshape(N_LAYER, N_TRACE, N_TRACE)
    place = jnp.arange(N_TRACE)
    forced = (orders == hotter[:, None, None]) | (orders == 0) | (orders == N_TRACE - 1)
    score = jnp.where(forced, -1, place[None, None, :])
    picked = jnp.argsort(score, axis=-1, stable=True)[..., :BLOCKS_DEV]
    owners = jnp.take_along_axis(orders, picked, axis=-1)
    local = jax.random.randint(jax.random.fold_in(base, 3), (N_LAYER, N_TRACE, BLOCKS_DEV), 0, BLK_DEV)
    sender = jnp.arange(N_TRACE)[None, :, None]
    local = jnp.where((sender == 0) & (owners == N_TRACE - 1), BLK_DEV - 1, local)
    local = jnp.where((sender == 0) & (owners == 0), 0, local)
    rows = owners * BLK_DEV + local
    col_local = jax.random.randint(jax.random.fold_in(base, 4), (N_LAYER, N_TRACE, BLOCKS_DEV), 0, BLK_DEV)
    which = jnp.arange(BLOCKS_DEV)[None, None, :]
    col_local = jnp.where((sender == 0) & (which == 0), 0, col_local)
    col_local = jnp.where((sender == N_TRACE - 1) & (which == 0), BLK_DEV - 1, col_local)
    cols = sender * BLK_DEV + col_local
    return (rows.astype(jnp.int32), cols.astype(jnp.int32))


def draw_row_block(key, part):
    return pattern(key)[0]


def draw_col_block(key, part):
    return pattern(key)[1]


def block_scale(own_key, dims, shards, least, largest):
    def one(position, parts):
        heights = jax.random.uniform(jax.random.fold_in(jax.random.fold_in(own_key, 6), position), (parts,), jnp.float32, least / len(shards), largest / len(shards))
        return jnp.repeat(jnp.exp(heights), dims[position] // parts).reshape((-1,) + (1,) * (len(dims) - position - 1))

    level = one(*shards[0])
    for cut in shards[1:]:
        level = level * one(*cut)
    return level


def gaussian(own_key, dims, scale, bound, cuts=(), held_as=jnp.bfloat16):
    loudness = block_scale(own_key, dims, cuts, -0.22, 0.18) if cuts else 1.0
    entries = jax.random.normal(own_key, dims, jnp.float32) * scale * loudness
    return jnp.minimum(jnp.maximum(entries, -bound), bound).astype(held_as)


def setup_inputs(seed: int = 0) -> dict:
    key_list = jax.random.split(jax.random.key(seed), 5)
    return {
        "operators": gaussian(key_list[0], (N_LAYERS, N_TRACE * BLOCKS_DEV, BLOCK, BLOCK), (BLOCK * max(1, BLOCKS_DEV * N_TRACE // (TRACE_ROWS // BLOCK))) ** -0.5, 0.25, ((0, 4), (1, 8))),
        "sources": gaussian(key_list[1], (N_LAYERS, BATCHES, TRACE_ROWS, SHOTS), 1.0, 6.0, ((0, 4), (2, 8))),
        "row_block": draw_row_block(jax.random.fold_in(key_list[4], 71), 0),
        "col_block": draw_col_block(jax.random.fold_in(key_list[4], 71), 0),
    }


def reference(operators, sources, row_block, col_block):
    count = TRACE_ROWS // BLOCK
    incoming = jnp.zeros((BATCHES, TRACE_ROWS, SHOTS), jnp.bfloat16)
    layers_out = []
    for layer in range(N_LAYERS):
        blocks = operators[layer].reshape(N_TRACE, BLOCKS_DEV, BLOCK, BLOCK)
        rows = row_block[layer].reshape(-1)
        cols = col_block[layer]
        outgoing = []
        for batch in range(BATCHES):
            field = (incoming[batch].astype(jnp.float32) + sources[layer, batch].astype(jnp.float32)).astype(jnp.bfloat16)
            tiles = field.reshape(count, BLOCK, SHOTS)

            def one_device(pair):
                mats, picks = pair
                pieces = tiles[picks]
                prod = jnp.einsum("kij,kjs->kis", mats.astype(jnp.float32), pieces.astype(jnp.float32))
                return prod.astype(jnp.bfloat16)

            prods = lax.map(one_device, (blocks, cols))
            summed = jax.ops.segment_sum(prods.reshape(-1, BLOCK, SHOTS).astype(jnp.float32), rows, num_segments=count)
            outgoing.append(summed.reshape(TRACE_ROWS, SHOTS).astype(jnp.bfloat16))
        incoming = jnp.stack(outgoing)
        layers_out.append(incoming)
    return jnp.stack(layers_out)
```

```python
import jax
import jax.numpy as jnp
from jax import lax
from jax.experimental import pallas as pl
from jax.experimental.pallas import tpu as pltpu
from jax.sharding import PartitionSpec as P


VMEM = pl.BlockSpec(memory_space=pltpu.VMEM)
SMEM = pl.BlockSpec(memory_space=pltpu.SMEM)
ANY = pl.BlockSpec(memory_space=pl.ANY)
LIMIT = 60 << 20


def section_kernel(senders, has_recv, has_out, *refs):
    state, slot_block, cols, match, source, blocks = refs[:6]
    refs = refs[6:]
    recv, refs = (refs[:senders], refs[senders:]) if has_recv else ((), refs)
    refs = refs[1:]
    slots, refs = (refs[:senders], refs[senders:]) if has_out else ((), refs)
    kept, pieces, total, made, in_sem, out_sem = refs
    place, batch, valid = state[0], state[1], state[2]
    stored = blocks.shape[0]

    def fetch(block):
        return pltpu.make_async_copy(
            source.at[batch, cols[block]], pieces.at[block], in_sem.at[block]
        )

    def keep(step, owner):
        return pltpu.make_async_copy(made.at[step], kept.at[owner, batch], out_sem.at[step])

    for block in range(stored):
        fetch(block).start()
    for block in range(stored):
        fetch(block).wait()
        if has_recv:
            count = match[0, block]
            for sender in range(1, senders):
                count += match[sender, block]

            @pl.when(count > 0)
            def _():
                total[...] = jnp.zeros_like(total)
                for step in range(senders):

                    @pl.when(match[lax.rem(place - step + senders, senders), block] > 0)
                    def _():
                        total[...] += recv[step][...].astype(jnp.float32)

                incoming = total[...].astype(jnp.bfloat16).astype(jnp.float32)
                pieces[block] = (incoming + pieces[block].astype(jnp.float32)).astype(jnp.bfloat16)

    for step in range(senders):
        owner = lax.rem(place + step, senders)
        block = slot_block[owner]

        @pl.when(block >= 0)
        def _():
            product = jnp.dot(
                blocks[block], pieces[block], preferred_element_type=jnp.float32
            ).astype(jnp.bfloat16)
            made[step] = product
            if has_out:
                slots[step][...] = product

            @pl.when(valid > 0)
            def _():
                keep(step, owner).start()

    for step in range(senders):
        owner = lax.rem(place + step, senders)

        @pl.when((slot_block[owner] >= 0) & (valid > 0))
        def _():
            keep(step, owner).wait()


def write_kernel(senders, rows_here, recv, out, total):
    group = out.shape[1]
    batch, first = pl.program_id(0), pl.program_id(1) * group
    for row in range(group):
        count = (rows_here[0] == first + row).astype(jnp.int32)
        for sender in range(1, senders):
            count += (rows_here[sender] == first + row).astype(jnp.int32)

        @pl.when(count == 0)
        def _():
            out[0, row] = jnp.zeros_like(out[0, row])

        @pl.when(count > 0)
        def _():
            total[...] = jnp.zeros_like(total)
            for sender in range(senders):

                @pl.when(rows_here[sender] == first + row)
                def _():
                    total[...] += recv[sender, batch].astype(jnp.float32)

            out[0, row] = total[...].astype(out.dtype)


def body(operators, sources, row_block, col_block):
    place = lax.axis_index("trace")
    depth = lax.axis_index("layer")
    senders = lax.axis_size("trace")
    layers = lax.axis_size("layer")
    blocks = operators[0]
    rows = row_block[0]
    stored, width = blocks.shape[0], blocks.shape[-1]
    batches, local, shots = sources.shape[1:]
    owned = local // width
    source = sources.reshape(batches, owned, width, shots)
    cols = col_block[0, 0]

    before = lax.ppermute(rows, "layer", [(i, i + 1) for i in range(layers - 1)])
    hits = (before[:, :, None] == cols[None, None, :]) & (depth > 0)
    match = jnp.max(hits.astype(jnp.int32), axis=1)
    mine = lax.dynamic_index_in_dim(rows, place, 0, keepdims=False)
    owners = jnp.arange(senders, dtype=jnp.int32)
    at = mine[None, :] // owned == owners[:, None]
    slot_block = jnp.sum(jnp.where(at, jnp.arange(stored, dtype=jnp.int32)[None, :] + 1, 0), axis=1) - 1
    here = rows // owned == place
    rows_here = jnp.sum(jnp.where(here, rows % owned + 1, 0), axis=1) - 1
    local_cols = cols - place * owned

    block_shape = jax.ShapeDtypeStruct((width, shots), jnp.bfloat16)
    kept_shape = jax.ShapeDtypeStruct((senders, batches, width, shots), jnp.bfloat16)
    kept = jnp.zeros(kept_shape.shape, kept_shape.dtype)
    recv = ()
    total_steps = layers + batches - 1
    for section in range(total_steps):
        which = section - depth
        valid = (which >= 0) & (which < batches)
        state = jnp.stack([place, jnp.clip(which, 0, batches - 1), valid.astype(jnp.int32)]).astype(jnp.int32)
        last = section + 1 == total_steps
        outs = (() if last else (block_shape,) * senders) + (kept_shape,)
        result = pl.pallas_call(
            lambda *refs, has_recv=bool(recv), has_out=not last: section_kernel(senders, has_recv, has_out, *refs),
            out_shape=outs,
            in_specs=[SMEM] * 4 + [ANY, VMEM] + [VMEM] * len(recv) + [ANY],
            out_specs=(() if last else (VMEM,) * senders) + (ANY,),
            scratch_shapes=[
                pltpu.VMEM((stored, width, shots), jnp.bfloat16),
                pltpu.VMEM((width, shots), jnp.float32),
                pltpu.VMEM((senders, width, shots), jnp.bfloat16),
                pltpu.SemaphoreType.DMA((stored,)),
                pltpu.SemaphoreType.DMA((senders,)),
            ],
            input_output_aliases={6 + len(recv): len(outs) - 1},
            compiler_params=pltpu.CompilerParams(vmem_limit_bytes=LIMIT),
            cost_estimate=pl.CostEstimate(
                flops=2 * stored * width * width * shots, bytes_accessed=8 << 20, transcendentals=0
            ),
            name="section",
        )(state, slot_block, local_cols, match, source, blocks, *recv, kept)
        kept = result[-1]
        if not last:
            froms = [i for i in range(layers - 1) if 0 <= section - i < batches]
            recv = tuple(
                lax.ppermute(
                    result[step],
                    ("layer", "trace"),
                    [
                        (i * senders + j, (i + 1) * senders + (j + step) % senders)
                        for i in froms
                        for j in range(senders)
                    ],
                )
                for step in range(senders)
            )
    arrived = lax.all_to_all(kept, "trace", split_axis=0, concat_axis=0, tiled=True)
    group = min(owned, 4)
    traces = pl.pallas_call(
        lambda *refs: write_kernel(senders, *refs),
        out_shape=jax.ShapeDtypeStruct((batches, owned, width, shots), jnp.bfloat16),
        grid=(batches, owned // group),
        in_specs=[SMEM, VMEM],
        out_specs=pl.BlockSpec((1, group, width, shots), lambda b, g: (b, g, 0, 0)),
        scratch_shapes=[pltpu.VMEM((width, shots), jnp.float32)],
        compiler_params=pltpu.CompilerParams(vmem_limit_bytes=LIMIT),
        name="write",
    )(rows_here, arrived)
    return traces.reshape(1, batches, local, shots)


def solution(mesh):
    placed = (
        P("layer", "trace", None, None),
        P("layer", None, "trace", None),
        P("layer", None, None),
        P("layer", "trace", None),
    )
    return jax.shard_map(
        body, mesh=mesh, in_specs=placed, out_specs=P("layer", None, "trace", None), check_vma=False
    )
```

```python
import jax
import jax.numpy as jnp
from jax import lax
from jax.experimental import pallas as pl
from jax.experimental.pallas import tpu as pltpu
from jax.sharding import PartitionSpec as P


SMEM = pl.BlockSpec(memory_space=pltpu.SMEM)
ANY = pl.BlockSpec(memory_space=pl.ANY)
LIMIT = 67043328


def product_kernel(layer, batch, owned, senders, has_recv, has_out, held, fresh, kept_at, *refs):
    state, rows, cols, source, blocks = refs[:5]
    refs = refs[5:]
    recv = ()
    if has_recv:
        before, recv, refs = refs[0], refs[1 : 1 + senders], refs[1 + senders :]
    refs = refs[held:]
    slots = ()
    if has_out:
        slots, refs = refs[:senders], refs[senders:]
    kept, refs = refs[kept_at], refs[fresh:]
    operand, pieces, arrived, total, made, from_row, op_sem, in_sem, recv_sem, out_sem, keep_sem = refs
    place = state[0]
    stored = blocks.shape[0]
    first = place * owned

    def load(block):
        return pltpu.make_async_copy(blocks.at[block], operand.at[block], op_sem.at[block])

    def fetch(block):
        return pltpu.make_async_copy(
            source.at[batch, cols[block] - first], pieces.at[block], in_sem.at[block]
        )

    def take(step):
        return pltpu.make_async_copy(recv[step], arrived.at[step], recv_sem.at[step])

    def give(step):
        return pltpu.make_async_copy(made.at[step], slots[step], out_sem.at[step])

    def keep(step, owner):
        return pltpu.make_async_copy(made.at[step], kept.at[owner], keep_sem.at[step])

    @pl.when(state[1] == layer)
    def _():
        for block in range(stored):
            fetch(block).start()
        for block in range(stored):
            load(block).start()
        if has_recv:
            for step in range(senders):
                sender = lax.rem(place - step + senders, senders)
                row = jnp.int32(-1)
                for other in range(stored):
                    value = before[sender, other]
                    row = jnp.where((value >= first) & (value < first + owned), value, row)
                hits = jnp.int32(0)
                for block in range(stored):
                    hits += (cols[block] == row).astype(jnp.int32)
                from_row[step] = jnp.where(hits > 0, row, -1)

                @pl.when(hits > 0)
                def _():
                    take(step).start()

            for step in range(senders):

                @pl.when(from_row[step] >= 0)
                def _():
                    take(step).wait()

        for block in range(stored):
            fetch(block).wait()
            if has_recv:
                count = jnp.int32(0)
                for step in range(senders):
                    count += (from_row[step] == cols[block]).astype(jnp.int32)

                @pl.when(count > 0)
                def _():
                    total[...] = jnp.zeros_like(total)
                    for step in range(senders):

                        @pl.when(from_row[step] == cols[block])
                        def _():
                            total[...] += arrived[step].astype(jnp.float32)

                    incoming = total[...].astype(jnp.bfloat16).astype(jnp.float32)
                    pieces[block] = (incoming + pieces[block].astype(jnp.float32)).astype(jnp.bfloat16)

        for block in range(stored):
            load(block).wait()

        def find(step):
            owner = lax.rem(place + step, senders)
            low = owner * owned
            block = jnp.int32(-1)
            for other in range(stored):
                value = rows[place, other]
                block = jnp.where((value >= low) & (value < low + owned), other, block)
            return owner, block

        @pl.loop(0, senders)
        def _(step):
            owner, block = find(step)
            from_row[step] = block

            @pl.when(block >= 0)
            def _():
                made[step] = jnp.dot(
                    operand[block], pieces[block], preferred_element_type=jnp.float32
                ).astype(jnp.bfloat16)
                keep(step, owner).start()
                for slot in range(senders if has_out else 0):

                    @pl.when(step == slot)
                    def _():
                        give(slot).start()

        for step in range(senders):

            @pl.when(from_row[step] >= 0)
            def _():
                if has_out:
                    give(step).wait()
                keep(step, 0).wait()


def hit_rows(rows, senders, place, owned, stored, here):
    first = place * owned
    for sender in range(senders):
        row = jnp.int32(-1)
        for other in range(stored):
            value = rows[sender, other] - first
            row = jnp.where((value >= 0) & (value < owned), value, row)
        here[sender] = row


def zero_kernel(owned, senders, stored, batches, state, rows, kept, out, nothing, here, sem):
    hit_rows(rows, senders, state[0], owned, stored, here)
    nothing[...] = jnp.zeros_like(nothing)

    def count(row):
        total = jnp.int32(0)
        for sender in range(senders):
            total += (here[sender] == row).astype(jnp.int32)
        return total

    def put(batch, row):
        return pltpu.make_async_copy(nothing, out.at[batch, row], sem.at[batch, row])

    @pl.loop(0, owned)
    def _(row):
        @pl.when(count(row) == 0)
        def _():
            for batch in range(batches):
                put(batch, row).start()

    @pl.loop(0, owned)
    def _(row):
        @pl.when(count(row) == 0)
        def _():
            for batch in range(batches):
                put(batch, row).wait()


def write_kernel(owned, senders, stored, batch, state, rows, recv, old, out, arrived, total, made, here, in_sem, out_sem):
    hit_rows(rows, senders, state[0], owned, stored, here)

    def take(sender):
        return pltpu.make_async_copy(recv.at[sender], arrived.at[sender], in_sem.at[sender])

    def put(sender):
        return pltpu.make_async_copy(made.at[sender], out.at[batch, here[sender]], out_sem.at[sender])

    def leads(sender):
        lead = here[sender] >= 0
        for other in range(sender):
            lead &= here[other] != here[sender]
        return lead

    for sender in range(senders):

        @pl.when(here[sender] >= 0)
        def _():
            take(sender).start()

    for sender in range(senders):

        @pl.when(here[sender] >= 0)
        def _():
            take(sender).wait()

    for sender in range(senders):

        @pl.when(leads(sender))
        def _():
            more = jnp.int32(0)
            for other in range(sender + 1, senders):
                more += (here[other] == here[sender]).astype(jnp.int32)

            @pl.when(more == 0)
            def _():
                made[sender] = arrived[sender]

            @pl.when(more > 0)
            def _():
                total[...] = arrived[sender].astype(jnp.float32)
                for other in range(sender + 1, senders):

                    @pl.when(here[other] == here[sender])
                    def _():
                        total[...] += arrived[other].astype(jnp.float32)

                made[sender] = total[...].astype(made.dtype)

            put(sender).start()

    for sender in range(senders):

        @pl.when(leads(sender))
        def _():
            put(sender).wait()


def body(operators, sources, row_block, col_block):
    place = lax.axis_index("trace")
    depth = lax.axis_index("layer")
    senders = lax.axis_size("trace")
    layers = lax.axis_size("layer")
    blocks = operators[0]
    rows = row_block[0]
    stored, width = blocks.shape[0], blocks.shape[-1]
    batches, local, shots = sources.shape[1:]
    owned = local // width
    source = sources.reshape(batches, owned, width, shots)
    cols = col_block[0, 0]
    state = jnp.stack([place, depth]).astype(jnp.int32)
    tile = (width, shots)
    dtype = sources.dtype
    params = pltpu.CompilerParams(vmem_limit_bytes=LIMIT)
    dma = pltpu.SemaphoreType.DMA

    def product(layer, batch, before, recv, kepts, kept_at, has_out):
        has_recv = before is not None
        slot_shapes = (jax.ShapeDtypeStruct(tile, dtype),) * senders if has_out else ()
        kept_shape = jax.ShapeDtypeStruct((senders,) + tile, dtype)
        extra = (before,) + tuple(recv) if has_recv else ()
        held = tuple(kepts)
        kept_outs = len(held) or batches
        outs = slot_shapes + (kept_shape,) * kept_outs
        result = pl.pallas_call(
            lambda *refs: product_kernel(
                layer, batch, owned, senders, has_recv, has_out, len(held), kept_outs, kept_at, *refs
            ),
            out_shape=outs,
            in_specs=[SMEM, SMEM, SMEM, ANY, ANY] + ([SMEM] + [ANY] * senders if has_recv else []) + [ANY] * len(held),
            out_specs=(ANY,) * len(outs),
            scratch_shapes=[
                pltpu.VMEM((stored, width, width), dtype),
                pltpu.VMEM((stored,) + tile, dtype),
                pltpu.VMEM((senders,) + tile, dtype),
                pltpu.VMEM(tile, jnp.float32),
                pltpu.VMEM((senders,) + tile, dtype),
                pltpu.SMEM((senders,), jnp.int32),
                dma((stored,)),
                dma((stored,)),
                dma((senders,)),
                dma((senders,)),
                dma((senders,)),
            ],
            input_output_aliases={
                5 + len(extra) + i: len(slot_shapes) + i for i in range(len(held))
            },
            compiler_params=params,
            cost_estimate=pl.CostEstimate(
                flops=2 * stored * width * width * shots, bytes_accessed=8 << 20, transcendentals=0
            ),
            name="product",
        )(state, rows, cols, source, blocks, *extra, *held)
        return result[: len(slot_shapes)], result[len(slot_shapes) :]

    def hop(layer, slots):
        return tuple(
            lax.ppermute(
                slots[step],
                ("layer", "trace"),
                [
                    (layer * senders + j, (layer + 1) * senders + (j + step) % senders)
                    for j in range(senders)
                ],
            )
            for step in range(senders)
        )

    kepts = ()
    recv = []
    for batch in range(batches):
        slots, kepts = product(0, batch, None, (), kepts, batch, layers > 1)
        recv.append(hop(0, slots) if layers > 1 else ())
    rows_after, kepts = lax.optimization_barrier((rows, kepts))
    before = lax.ppermute(rows_after, "layer", [(i, i + 1) for i in range(layers - 1)])

    traces = None
    for layer in range(1, layers):
        last = layer + 1 == layers
        for batch in range(batches):
            if last:
                slots, (new,) = product(layer, batch, before, recv[batch], (kepts[batch],), 0, False)
                kepts = tuple(new if i == batch else k for i, k in enumerate(kepts))
            else:
                slots, kepts = product(layer, batch, before, recv[batch], kepts, batch, True)
                recv[batch] = hop(layer, slots)
        if layer == 1:
            traces = pl.pallas_call(
                lambda *refs: zero_kernel(owned, senders, stored, batches, *refs),
                out_shape=jax.ShapeDtypeStruct((batches, owned) + tile, dtype),
                in_specs=[SMEM, SMEM, ANY],
                out_specs=ANY,
                scratch_shapes=[
                    pltpu.VMEM(tile, dtype),
                    pltpu.SMEM((senders,), jnp.int32),
                    dma((batches, owned)),
                ],
                compiler_params=params,
                name="zeros",
            )(state, rows, kepts[0])
    for batch in range(batches):
        arrived = lax.all_to_all(kepts[batch], "trace", split_axis=0, concat_axis=0, tiled=True)
        traces = pl.pallas_call(
            lambda *refs, batch=batch: write_kernel(owned, senders, stored, batch, *refs),
            out_shape=jax.ShapeDtypeStruct((batches, owned) + tile, dtype),
            in_specs=[SMEM, SMEM, ANY, ANY],
            out_specs=ANY,
            scratch_shapes=[
                pltpu.VMEM((senders,) + tile, dtype),
                pltpu.VMEM(tile, jnp.float32),
                pltpu.VMEM((senders,) + tile, dtype),
                pltpu.SMEM((senders,), jnp.int32),
                dma((senders,)),
                dma((senders,)),
            ],
            input_output_aliases={3: 0},
            compiler_params=params,
            name="write",
        )(state, rows, arrived, traces)
    return traces.reshape(1, batches, local, shots)


def solution(mesh):
    placed = (
        P("layer", "trace", None, None),
        P("layer", None, "trace", None),
        P("layer", None, None),
        P("layer", "trace", None),
    )
    return jax.shard_map(
        body, mesh=mesh, in_specs=placed, out_specs=P("layer", None, "trace", None), check_vma=False
    )
```

```python
import jax
import jax.numpy as jnp
from jax import lax
from jax.experimental import pallas as pl
from jax.experimental.pallas import tpu as pltpu
from jax.sharding import PartitionSpec as P


AXES = ("layer", "trace")
SMEM = pl.BlockSpec(memory_space=pltpu.SMEM)
ANY = pl.BlockSpec(memory_space=pl.ANY)
PARAMS = pltpu.CompilerParams(vmem_limit_bytes=67043328)
DMA = pltpu.SemaphoreType.DMA


def owner_of(row, owned):
    if owned & (owned - 1) == 0:
        return lax.shift_right_logical(row, jnp.int32(owned.bit_length() - 1))
    return lax.div(row, jnp.int32(owned))


def first_kernel(senders, owned, state, rows, cols, source, blocks, *refs):
    slots, refs = refs[:senders], refs[senders:]
    kept, operand, pieces, made, op_sem, in_sem, slot_sem, keep_sem = refs
    place = state[0]
    stored, width = blocks.shape[:2]
    batches, shots = source.shape[0], source.shape[-1]

    def load(block):
        return pltpu.make_async_copy(blocks.at[block], operand.at[block], op_sem.at[block])

    def fetch(block, batch):
        return pltpu.make_async_copy(
            source.at[batch, cols[block] - place * owned],
            pieces.at[block, :, pl.ds(batch * shots, shots)],
            in_sem.at[block, batch],
        )

    def give(block, slot):
        return pltpu.make_async_copy(made.at[block], slots[slot], slot_sem.at[block])

    def keep(block, owner):
        return pltpu.make_async_copy(made.at[block], kept.at[owner], keep_sem.at[block])

    @pl.loop(0, stored)
    def _(block):
        for batch in range(batches):
            fetch(block, batch).start()
        load(block).start()

    @pl.loop(0, stored)
    def _(block):
        for batch in range(batches):
            fetch(block, batch).wait()
        load(block).wait()
        product = jnp.dot(operand[block], pieces[block], preferred_element_type=jnp.float32)
        for batch in range(batches):
            made[block, batch] = product[:, batch * shots : (batch + 1) * shots].astype(made.dtype)
        owner = owner_of(rows[place, block], owned)
        shift = lax.rem(owner - place + senders, senders)
        for slot in range(senders):

            @pl.when(shift == slot)
            def _():
                give(block, slot).start()

        keep(block, owner).start()

    @pl.loop(0, stored)
    def _(block):
        give(block, 0).wait()
        keep(block, 0).wait()


def renew_kernel(senders, owned, has_fresh, state, rows, cols, match, flags, source, blocks, *refs):
    recv, refs = refs[:senders], refs[senders:]
    if has_fresh:
        fresh, refs = refs[0], refs[1:]
    kept, operand, pieces, arrived, total, made, op_sem, in_sem, recv_sem, keep_sem = refs[1:]
    place = state[0]
    stored, width = blocks.shape[:2]
    batches, shots = source.shape[0], source.shape[-1]
    go = flags[senders] > 0

    def load(block):
        return pltpu.make_async_copy(blocks.at[block], operand.at[block], op_sem.at[block])

    def fetch(block, batch):
        return pltpu.make_async_copy(
            source.at[batch, cols[block] - place * owned],
            pieces.at[block, :, pl.ds(batch * shots, shots)],
            in_sem.at[block, batch],
        )

    def take(step):
        return pltpu.make_async_copy(recv[step], arrived.at[step], recv_sem.at[step])

    def keep(block, owner):
        return pltpu.make_async_copy(made.at[block], kept.at[owner], keep_sem.at[block])

    def hits(block):
        return match[block, senders]

    def sender_at(step):
        return lax.rem(place - step + senders, senders)

    @pl.when(go)
    def _():
        for step in range(senders):

            @pl.when(match[stored, sender_at(step)] > 0)
            def _():
                if has_fresh:

                    @pl.when(flags[step] > 0)
                    def _():
                        pltpu.make_async_copy(fresh.at[step], arrived.at[step], recv_sem.at[step]).start()

                    @pl.when(flags[step] == 0)
                    def _():
                        take(step).start()

                else:
                    take(step).start()

        @pl.loop(0, stored)
        def _(block):
            @pl.when(hits(block) > 0)
            def _():
                for batch in range(batches):
                    fetch(block, batch).start()
                load(block).start()

        for step in range(senders):

            @pl.when(match[stored, sender_at(step)] > 0)
            def _():
                take(step).wait()

        @pl.loop(0, stored)
        def _(block):
            @pl.when(hits(block) > 0)
            def _():
                total[...] = jnp.zeros_like(total)

                @pl.loop(0, senders)
                def _(step):
                    @pl.when(match[block, sender_at(step)] > 0)
                    def _():
                        total[...] += arrived[step].astype(jnp.float32)

                for batch in range(batches):
                    fetch(block, batch).wait()
                for batch in range(batches):
                    lanes = pl.ds(batch * shots, shots)
                    incoming = total[batch].astype(pieces.dtype).astype(jnp.float32)
                    pieces[block, :, lanes] = (
                        incoming + pieces[block, :, lanes].astype(jnp.float32)
                    ).astype(pieces.dtype)
                load(block).wait()
                product = jnp.dot(operand[block], pieces[block], preferred_element_type=jnp.float32)
                for batch in range(batches):
                    made[block, batch] = product[:, batch * shots : (batch + 1) * shots].astype(made.dtype)
                keep(block, owner_of(rows[place, block], owned)).start()

        @pl.loop(0, stored)
        def _(block):
            @pl.when(hits(block) > 0)
            def _():
                keep(block, 0).wait()


def hit_rows(rows, senders, place, owned, stored, here):
    first = place * owned

    @pl.loop(0, senders)
    def _(sender):
        row = jnp.int32(-1)
        for other in range(stored):
            value = rows[sender, other] - first
            row = jnp.where((value >= 0) & (value < owned), value, row)
        here[sender] = row


def zero_kernel(owned, senders, stored, batches, state, rows, after, out, nothing, here, sem):
    hit_rows(rows, senders, state[0], owned, stored, here)
    nothing[...] = jnp.zeros_like(nothing)

    def free(row):
        total = jnp.int32(0)
        for sender in range(senders):
            total += (here[sender] == row).astype(jnp.int32)
        return total == 0

    def put(batch, row):
        return pltpu.make_async_copy(nothing, out.at[batch, row], sem.at[batch, row])

    @pl.loop(0, owned)
    def _(row):
        @pl.when(free(row))
        def _():
            for batch in range(batches):
                put(batch, row).start()

    @pl.loop(0, owned)
    def _(row):
        @pl.when(free(row))
        def _():
            for batch in range(batches):
                put(batch, row).wait()


def write_kernel(owned, senders, stored, batches, state, rows, recv, old, out, arrived, total, made, here, in_sem, out_sem):
    hit_rows(rows, senders, state[0], owned, stored, here)

    def take(sender):
        return pltpu.make_async_copy(recv.at[sender], arrived.at[sender], in_sem.at[sender])

    def put(sender, batch, box):
        return pltpu.make_async_copy(box.at[sender, batch], out.at[batch, here[sender]], out_sem.at[sender, batch])

    def count(sender, first, last):
        total = jnp.int32(0)
        for other in range(senders):
            same = (here[other] == here[sender]) & (other >= first) & (other < last)
            total += same.astype(jnp.int32)
        return total

    @pl.loop(0, senders)
    def _(sender):
        @pl.when(here[sender] >= 0)
        def _():
            take(sender).start()

    @pl.loop(0, senders)
    def _(sender):
        @pl.when(here[sender] >= 0)
        def _():
            take(sender).wait()

    @pl.loop(0, senders)
    def _(sender):
        @pl.when((here[sender] >= 0) & (count(sender, 0, sender) == 0))
        def _():
            more = count(sender, sender + 1, senders)

            @pl.when(more == 0)
            def _():
                for batch in range(batches):
                    put(sender, batch, arrived).start()

            @pl.when(more > 0)
            def _():
                total[...] = arrived[sender].astype(jnp.float32)

                @pl.loop(sender + 1, senders)
                def _(other):
                    @pl.when(here[other] == here[sender])
                    def _():
                        total[...] += arrived[other].astype(jnp.float32)

                made[sender] = total[...].astype(made.dtype)
                for batch in range(batches):
                    put(sender, batch, made).start()

    @pl.loop(0, senders)
    def _(sender):
        @pl.when((here[sender] >= 0) & (count(sender, 0, sender) == 0))
        def _():
            for batch in range(batches):
                put(sender, batch, made).wait()


def body(operators, sources, row_block, col_block):
    place = lax.axis_index("trace")
    depth = lax.axis_index("layer")
    senders = lax.axis_size("trace")
    layers = lax.axis_size("layer")
    blocks = operators[0]
    rows = row_block[0]
    stored, width = blocks.shape[0], blocks.shape[-1]
    batches, local, shots = sources.shape[1:]
    owned = local // width
    source = sources.reshape(batches, owned, width, shots)
    cols = col_block[0, 0]
    state = jnp.stack([place, depth]).astype(jnp.int32)
    dtype = sources.dtype
    tile = (batches, width, shots)
    slot = jax.ShapeDtypeStruct(tile, dtype)
    held = jax.ShapeDtypeStruct((senders,) + tile, dtype)

    def pairs(step):
        return [
            (i * senders + j, (i + 1) * senders + (j + step) % senders)
            for i in range(layers - 1)
            for j in range(senders)
        ]

    *slots, kept = pl.pallas_call(
        lambda *refs: first_kernel(senders, owned, *refs),
        out_shape=(slot,) * senders + (held,),
        in_specs=[SMEM] * 3 + [ANY] * 2,
        out_specs=(ANY,) * (senders + 1),
        scratch_shapes=[
            pltpu.VMEM((stored, width, width), dtype),
            pltpu.VMEM((stored, width, batches * shots), dtype),
            pltpu.VMEM((stored,) + tile, dtype),
            DMA((stored,)),
            DMA((stored, batches)),
            DMA((stored,)),
            DMA((stored,)),
        ],
        compiler_params=PARAMS,
        name="first",
    )(state, rows, cols, source, blocks)
    recv = [lax.ppermute(slots[step], AXES, pairs(step)) for step in range(senders)]

    total = layers * senders
    mine = jnp.concatenate([rows.reshape(-1), cols])
    mine, kept = lax.optimization_barrier((mine, kept))
    known = lax.all_to_all(
        jnp.broadcast_to(mine[None], (total, mine.shape[0])), AXES, split_axis=0, concat_axis=0, tiled=True
    ).reshape(layers, senders, -1)
    blocks_all = senders * stored
    rows_all = known[:, 0, :blocks_all]
    cols_all = known[:, :, blocks_all:].reshape(layers, blocks_all)
    feeds = rows_all[:-1, :, None] == cols_all[1:, None, :]
    read = jnp.any(feeds, axis=2)
    home = jnp.repeat(jnp.arange(senders, dtype=jnp.int32), stored)
    shift = (rows_all[:-1] // owned - home[None, :]) % senders
    steps = jnp.arange(senders, dtype=jnp.int32)
    changed = jnp.any(feeds, axis=1)
    lists, masks = [], []
    for wave in range(2, layers):
        below = jnp.concatenate([jnp.zeros((1, blocks_all), bool), changed[:-1]])
        again = below & read
        mask = jnp.any(again[:, :, None] & (shift[:, :, None] == steps), axis=(0, 1)).astype(jnp.int32)
        order = jnp.sum(
            jnp.where(
                (jnp.cumsum(mask)[None, :] == steps[:, None] + 1) & (mask[None, :] > 0), steps[None, :], 0
            ),
            axis=1,
        )
        lists.append((order, jnp.sum(mask)))
        masks.append(mask)
        changed = jnp.any(feeds & below[:, :, None], axis=1)

    above = lax.dynamic_index_in_dim(rows_all, jnp.maximum(depth - 1, 0), 0, keepdims=False)
    above = above.reshape(senders, stored)
    match = jnp.any((above[None] == cols[:, None, None]) & (depth > 0), axis=2).astype(jnp.int32)
    match = jnp.concatenate([match, jnp.max(match, axis=0, keepdims=True)])
    match = jnp.concatenate([match, jnp.max(match, axis=1, keepdims=True)], axis=1)

    def renew(kept, fresh, flags):
        held_fresh = () if fresh is None else (fresh,)
        return pl.pallas_call(
            lambda *refs: renew_kernel(senders, owned, fresh is not None, *refs),
            out_shape=held,
            in_specs=[SMEM] * 5 + [ANY] * (3 + senders + len(held_fresh)),
            out_specs=ANY,
            scratch_shapes=[
                pltpu.VMEM((stored, width, width), dtype),
                pltpu.VMEM((stored, width, batches * shots), dtype),
                pltpu.VMEM((senders,) + tile, dtype),
                pltpu.VMEM(tile, jnp.float32),
                pltpu.VMEM((stored,) + tile, dtype),
                DMA((stored,)),
                DMA((stored, batches)),
                DMA((senders,)),
                DMA((stored,)),
            ],
            input_output_aliases={7 + senders + len(held_fresh): 0},
            compiler_params=PARAMS,
            name="renew",
        )(state, rows, cols, match, flags, source, blocks, *recv, *held_fresh, kept)

    traces = pl.pallas_call(
        lambda *refs: zero_kernel(owned, senders, stored, batches, *refs),
        out_shape=jax.ShapeDtypeStruct((batches, owned, width, shots), dtype),
        in_specs=[SMEM, SMEM, ANY],
        out_specs=ANY,
        scratch_shapes=[
            pltpu.VMEM((width, shots), dtype),
            pltpu.SMEM((senders,), jnp.int32),
            DMA((batches, owned)),
        ],
        compiler_params=PARAMS,
        name="zeros",
    )(state, rows, recv[0])

    kept = renew(kept, None, jnp.ones((senders + 1,), jnp.int32))
    fresh = jnp.zeros(held.shape, dtype)
    seen = jnp.zeros((senders,), jnp.int32)
    for (order, count), mask in zip(lists, masks):

        def resend(carry):
            done, fresh = carry
            step = lax.dynamic_index_in_dim(order, done, 0, keepdims=False)
            sent = lax.dynamic_index_in_dim(kept, (place + step) % senders, 0, keepdims=False)
            came = lax.switch(
                step, [lambda x, step=step: lax.ppermute(x, AXES, pairs(step)) for step in range(senders)], sent
            )
            return done + 1, lax.dynamic_update_index_in_dim(fresh, came, step, 0)

        _, fresh = lax.while_loop(lambda carry: carry[0] < count, resend, (jnp.int32(0), fresh))
        seen = jnp.maximum(seen, mask)
        kept = renew(kept, fresh, jnp.concatenate([seen, count[None]]))

    arrived = lax.all_to_all(kept, "trace", split_axis=0, concat_axis=0, tiled=True)
    traces = pl.pallas_call(
        lambda *refs: write_kernel(owned, senders, stored, batches, *refs),
        out_shape=jax.ShapeDtypeStruct((batches, owned, width, shots), dtype),
        in_specs=[SMEM, SMEM, ANY, ANY],
        out_specs=ANY,
        scratch_shapes=[
            pltpu.VMEM((senders,) + tile, dtype),
            pltpu.VMEM(tile, jnp.float32),
            pltpu.VMEM((senders,) + tile, dtype),
            pltpu.SMEM((senders,), jnp.int32),
            DMA((senders,)),
            DMA((senders, batches)),
        ],
        input_output_aliases={3: 0},
        compiler_params=PARAMS,
        name="write",
    )(state, rows, arrived, traces)
    return traces.reshape(1, batches, local, shots)


def solution(mesh):
    placed = (
        P("layer", "trace", None, None),
        P("layer", None, "trace", None),
        P("layer", None, None),
        P("layer", "trace", None),
    )
    return jax.shard_map(
        body, mesh=mesh, in_specs=placed, out_specs=P("layer", None, "trace", None), check_vma=False
    )
```

```python
import jax
import jax.numpy as jnp
from jax import lax
from jax.experimental import pallas as pl
from jax.experimental.pallas import tpu as pltpu
from jax.sharding import PartitionSpec as P


AXES = ("layer", "trace")
SMEM = pl.BlockSpec(memory_space=pltpu.SMEM)
ANY = pl.BlockSpec(memory_space=pl.ANY)
PARAMS = pltpu.CompilerParams(vmem_limit_bytes=67043328)
DMA = pltpu.SemaphoreType.DMA


def owner_of(row, owned):
    if owned & (owned - 1) == 0:
        return lax.shift_right_logical(row, jnp.int32(owned.bit_length() - 1))
    return lax.div(row, jnp.int32(owned))


def first_kernel(senders, owned, state, rows, cols, source, blocks, *refs):
    slots, refs = refs[:senders], refs[senders:]
    kept, operand, pieces, made, op_sem, in_sem, slot_sem, keep_sem = refs
    place = state[0]
    stored, _ = blocks.shape[:2]
    batches, shots = source.shape[0], source.shape[-1]

    def load(block):
        return pltpu.make_async_copy(blocks.at[block], operand.at[block], op_sem.at[block])

    def fetch(block, batch):
        return pltpu.make_async_copy(
            source.at[batch, cols[block] - place * owned],
            pieces.at[block, :, pl.ds(batch * shots, shots)],
            in_sem.at[block, batch],
        )

    def give(block, slot):
        return pltpu.make_async_copy(made.at[block], slots[slot], slot_sem.at[block])

    def keep(block, owner):
        return pltpu.make_async_copy(made.at[block], kept.at[owner], keep_sem.at[block])

    @pl.loop(0, stored)
    def _(block):
        for batch in range(batches):
            fetch(block, batch).start()
        load(block).start()

    @pl.loop(0, stored)
    def _(block):
        for batch in range(batches):
            fetch(block, batch).wait()
        load(block).wait()
        product = jnp.dot(operand[block], pieces[block], preferred_element_type=jnp.float32)
        for batch in range(batches):
            made[block, batch] = product[:, batch * shots : (batch + 1) * shots].astype(made.dtype)
        owner = owner_of(rows[place, block], owned)
        shift = lax.rem(owner - place + senders, senders)
        for slot in range(senders):

            @pl.when(shift == slot)
            def _():
                give(block, slot).start()

        keep(block, owner).start()

    @pl.loop(0, stored)
    def _(block):
        give(block, 0).wait()
        keep(block, 0).wait()


def renew_kernel(senders, owned, state, rows, cols, match, go, source, blocks, *refs):
    recv, refs = refs[:senders], refs[senders:]
    kept, operand, pieces, arrived, total, made, op_sem, in_sem, recv_sem, keep_sem = refs[1:]
    place = state[0]
    stored, _ = blocks.shape[:2]
    batches, shots = source.shape[0], source.shape[-1]

    def load(block):
        return pltpu.make_async_copy(blocks.at[block], operand.at[block], op_sem.at[block])

    def fetch(block, batch):
        return pltpu.make_async_copy(
            source.at[batch, cols[block] - place * owned],
            pieces.at[block, :, pl.ds(batch * shots, shots)],
            in_sem.at[block, batch],
        )

    def take(step):
        return pltpu.make_async_copy(recv[step], arrived.at[step], recv_sem.at[step])

    def keep(block, owner):
        return pltpu.make_async_copy(made.at[block], kept.at[owner], keep_sem.at[block])

    def hits(block):
        return match[block, senders]

    def sender_at(step):
        return lax.rem(place - step + senders, senders)

    @pl.when(go[0] > 0)
    def _():
        for step in range(senders):

            @pl.when(match[stored, sender_at(step)] > 0)
            def _():
                take(step).start()

        @pl.loop(0, stored)
        def _(block):
            @pl.when(hits(block) > 0)
            def _():
                for batch in range(batches):
                    fetch(block, batch).start()
                load(block).start()

        for step in range(senders):

            @pl.when(match[stored, sender_at(step)] > 0)
            def _():
                take(step).wait()

        @pl.loop(0, stored)
        def _(block):
            @pl.when(hits(block) > 0)
            def _():
                total[...] = jnp.zeros_like(total)

                @pl.loop(0, senders)
                def _(step):
                    @pl.when(match[block, sender_at(step)] > 0)
                    def _():
                        total[...] += arrived[step].astype(jnp.float32)

                for batch in range(batches):
                    fetch(block, batch).wait()
                for batch in range(batches):
                    lanes = pl.ds(batch * shots, shots)
                    incoming = total[batch].astype(pieces.dtype).astype(jnp.float32)
                    pieces[block, :, lanes] = (
                        incoming + pieces[block, :, lanes].astype(jnp.float32)
                    ).astype(pieces.dtype)
                load(block).wait()
                product = jnp.dot(operand[block], pieces[block], preferred_element_type=jnp.float32)
                for batch in range(batches):
                    made[block, batch] = product[:, batch * shots : (batch + 1) * shots].astype(made.dtype)
                keep(block, owner_of(rows[place, block], owned)).start()

        @pl.loop(0, stored)
        def _(block):
            @pl.when(hits(block) > 0)
            def _():
                keep(block, 0).wait()


def hit_rows(rows, senders, place, owned, stored, here):
    first = place * owned

    @pl.loop(0, senders)
    def _(sender):
        row = jnp.int32(-1)
        for other in range(stored):
            value = rows[sender, other] - first
            row = jnp.where((value >= 0) & (value < owned), value, row)
        here[sender] = row


def zero_kernel(owned, senders, stored, batches, state, rows, after, out, nothing, here, sem):
    hit_rows(rows, senders, state[0], owned, stored, here)
    nothing[...] = jnp.zeros_like(nothing)

    def free(row):
        total = jnp.int32(0)
        for sender in range(senders):
            total += (here[sender] == row).astype(jnp.int32)
        return total == 0

    def put(batch, row):
        return pltpu.make_async_copy(nothing, out.at[batch, row], sem.at[batch, row])

    @pl.loop(0, owned)
    def _(row):
        @pl.when(free(row))
        def _():
            for batch in range(batches):
                put(batch, row).start()

    @pl.loop(0, owned)
    def _(row):
        @pl.when(free(row))
        def _():
            for batch in range(batches):
                put(batch, row).wait()


def write_kernel(owned, senders, stored, batches, state, rows, recv, old, out, arrived, total, made, here, in_sem, out_sem):
    hit_rows(rows, senders, state[0], owned, stored, here)

    def take(sender):
        return pltpu.make_async_copy(recv.at[sender], arrived.at[sender], in_sem.at[sender])

    def put(sender, batch, box):
        return pltpu.make_async_copy(box.at[sender, batch], out.at[batch, here[sender]], out_sem.at[sender, batch])

    def count(sender, first, last):
        total = jnp.int32(0)
        for other in range(senders):
            same = (here[other] == here[sender]) & (other >= first) & (other < last)
            total += same.astype(jnp.int32)
        return total

    @pl.loop(0, senders)
    def _(sender):
        @pl.when(here[sender] >= 0)
        def _():
            take(sender).start()

    @pl.loop(0, senders)
    def _(sender):
        @pl.when(here[sender] >= 0)
        def _():
            take(sender).wait()

    @pl.loop(0, senders)
    def _(sender):
        @pl.when((here[sender] >= 0) & (count(sender, 0, sender) == 0))
        def _():
            more = count(sender, sender + 1, senders)

            @pl.when(more == 0)
            def _():
                for batch in range(batches):
                    put(sender, batch, arrived).start()

            @pl.when(more > 0)
            def _():
                total[...] = arrived[sender].astype(jnp.float32)

                @pl.loop(sender + 1, senders)
                def _(other):
                    @pl.when(here[other] == here[sender])
                    def _():
                        total[...] += arrived[other].astype(jnp.float32)

                made[sender] = total[...].astype(made.dtype)
                for batch in range(batches):
                    put(sender, batch, made).start()

    @pl.loop(0, senders)
    def _(sender):
        @pl.when((here[sender] >= 0) & (count(sender, 0, sender) == 0))
        def _():
            for batch in range(batches):
                put(sender, batch, made).wait()


def body(operators, sources, row_block, col_block):
    place = lax.axis_index("trace")
    depth = lax.axis_index("layer")
    senders = lax.axis_size("trace")
    layers = lax.axis_size("layer")
    blocks = operators[0]
    rows = row_block[0]
    stored, width = blocks.shape[0], blocks.shape[-1]
    batches, local, shots = sources.shape[1:]
    owned = local // width
    source = sources.reshape(batches, owned, width, shots)
    cols = col_block[0, 0]
    state = jnp.stack([place, depth]).astype(jnp.int32)
    dtype = sources.dtype
    tile = (batches, width, shots)
    slot = jax.ShapeDtypeStruct(tile, dtype)
    held = jax.ShapeDtypeStruct((senders,) + tile, dtype)

    def pairs(step):
        return [
            (i * senders + j, (i + 1) * senders + (j + step) % senders)
            for i in range(layers - 1)
            for j in range(senders)
        ]

    *slots, kept = pl.pallas_call(
        lambda *refs: first_kernel(senders, owned, *refs),
        out_shape=(slot,) * senders + (held,),
        in_specs=[SMEM] * 3 + [ANY] * 2,
        out_specs=(ANY,) * (senders + 1),
        scratch_shapes=[
            pltpu.VMEM((stored, width, width), dtype),
            pltpu.VMEM((stored, width, batches * shots), dtype),
            pltpu.VMEM((stored,) + tile, dtype),
            DMA((stored,)),
            DMA((stored, batches)),
            DMA((stored,)),
            DMA((stored,)),
        ],
        compiler_params=PARAMS,
        name="first",
    )(state, rows, cols, source, blocks)
    recv = []
    for step in range(senders):
        recv.append(lax.ppermute(slots[step], AXES, pairs(step)))

    total = layers * senders
    mine = jnp.concatenate([rows.reshape(-1), cols])
    mine, kept = lax.optimization_barrier((mine, kept))
    mine = jnp.broadcast_to(mine[None], (total, mine.shape[0]))
    known = lax.all_to_all(mine, AXES, split_axis=0, concat_axis=0, tiled=True)
    known = known.reshape(layers, senders, -1)
    blocks_all = senders * stored
    rows_all = known[:, 0, :blocks_all]
    cols_all = known[:, :, blocks_all:].reshape(layers, blocks_all)
    feeds = rows_all[:-1, :, None] == cols_all[1:, None, :]
    read = jnp.any(feeds, axis=2)
    home = jnp.repeat(jnp.arange(senders, dtype=jnp.int32), stored)
    shift = (rows_all[:-1] // owned - home[None, :]) % senders
    steps = jnp.arange(senders, dtype=jnp.int32)
    changed = jnp.any(feeds, axis=1)
    masks = []
    group = 4 if senders <= 8 else 2
    for _ in range(2, layers):
        below = jnp.concatenate([jnp.zeros((1, blocks_all), bool), changed[:-1]])
        again = below & read
        mask = jnp.any(again[:, :, None] & (shift[:, :, None] == steps), axis=(0, 1)).astype(jnp.int32)
        masks.append(mask)
        changed = jnp.any(feeds & below[:, :, None], axis=1)

    above = lax.dynamic_index_in_dim(rows_all, jnp.maximum(depth - 1, 0), 0, keepdims=False)
    above = above.reshape(senders, stored)
    match = jnp.any((above[None] == cols[:, None, None]) & (depth > 0), axis=2).astype(jnp.int32)
    match = jnp.concatenate([match, jnp.max(match, axis=0, keepdims=True)])
    match = jnp.concatenate([match, jnp.max(match, axis=1, keepdims=True)], axis=1)

    def renew(kept, go):
        return pl.pallas_call(
            lambda *refs: renew_kernel(senders, owned, *refs),
            out_shape=held,
            in_specs=[SMEM] * 5 + [ANY] * (3 + senders),
            out_specs=ANY,
            scratch_shapes=[
                pltpu.VMEM((stored, width, width), dtype),
                pltpu.VMEM((stored, width, batches * shots), dtype),
                pltpu.VMEM((senders,) + tile, dtype),
                pltpu.VMEM(tile, jnp.float32),
                pltpu.VMEM((stored,) + tile, dtype),
                DMA((stored,)),
                DMA((stored, batches)),
                DMA((senders,)),
                DMA((stored,)),
            ],
            input_output_aliases={7 + senders: 0},
            compiler_params=PARAMS,
            name="renew",
        )(state, rows, cols, match, go[None], source, blocks, *recv, kept)

    traces = pl.pallas_call(
        lambda *refs: zero_kernel(owned, senders, stored, batches, *refs),
        out_shape=jax.ShapeDtypeStruct((batches, owned, width, shots), dtype),
        in_specs=[SMEM, SMEM, ANY],
        out_specs=ANY,
        scratch_shapes=[
            pltpu.VMEM((width, shots), dtype),
            pltpu.SMEM((senders,), jnp.int32),
            DMA((batches, owned)),
        ],
        compiler_params=PARAMS,
        name="zeros",
    )(state, rows, recv[0])

    kept = renew(kept, jnp.int32(1))

    def again(step, kept):
        sent = lax.dynamic_index_in_dim(kept, (place + step) % senders, 0, keepdims=False)
        return lax.ppermute(sent, AXES, pairs(step))

    for wave, mask in enumerate(masks):
        if wave == 0:
            for low in range(0, senders, group):
                near = range(low, min(low + group, senders))

                def resend(which):
                    return lambda kept, old: tuple(
                        again(step, kept) if which >> at & 1 else old[at] for at, step in enumerate(near)
                    )

                code = sum(mask[step] << at for at, step in enumerate(near))
                recv[low : low + group] = lax.switch(
                    code, [resend(which) for which in range(1 << len(near))], kept, tuple(recv[low : low + group])
                )
        else:

            def resend_one(carry):
                left, recv = carry
                step = jnp.argmax(left).astype(jnp.int32)
                recv = lax.switch(
                    step,
                    [
                        lambda kept, recv, step=step: recv[:step] + (again(step, kept),) + recv[step + 1 :]
                        for step in range(senders)
                    ],
                    kept,
                    recv,
                )
                return jnp.where(steps == step, 0, left), recv

            recv = list(lax.while_loop(lambda carry: jnp.max(carry[0]) > 0, resend_one, (mask, tuple(recv)))[1])
        kept = renew(kept, jnp.max(mask))

    arrived = lax.all_to_all(kept, "trace", split_axis=0, concat_axis=0, tiled=True)
    traces = pl.pallas_call(
        lambda *refs: write_kernel(owned, senders, stored, batches, *refs),
        out_shape=jax.ShapeDtypeStruct((batches, owned, width, shots), dtype),
        in_specs=[SMEM, SMEM, ANY, ANY],
        out_specs=ANY,
        scratch_shapes=[
            pltpu.VMEM((senders,) + tile, dtype),
            pltpu.VMEM(tile, jnp.float32),
            pltpu.VMEM((senders,) + tile, dtype),
            pltpu.SMEM((senders,), jnp.int32),
            DMA((senders,)),
            DMA((senders, batches)),
        ],
        input_output_aliases={3: 0},
        compiler_params=PARAMS,
        name="write",
    )(state, rows, arrived, traces)
    return traces.reshape(1, batches, local, shots)


def solution(mesh):
    placed = (
        P("layer", "trace", None, None),
        P("layer", None, "trace", None),
        P("layer", None, None),
        P("layer", "trace", None),
    )
    return jax.shard_map(
        body, mesh=mesh, in_specs=placed, out_specs=P("layer", None, "trace", None), check_vma=False
    )
```

```python
import jax
import jax.numpy as jnp
from jax import lax
from jax.experimental import pallas as pl
from jax.experimental.pallas import tpu as pltpu
from jax.sharding import PartitionSpec as P


AXES = ("layer", "trace")
SMEM = pl.BlockSpec(memory_space=pltpu.SMEM)
ANY = pl.BlockSpec(memory_space=pl.ANY)
PARAMS = pltpu.CompilerParams(vmem_limit_bytes=67043328)
DMA = pltpu.SemaphoreType.DMA


def owner_of(row, owned):
    if owned & (owned - 1) == 0:
        return lax.shift_right_logical(row, jnp.int32(owned.bit_length() - 1))
    return lax.div(row, jnp.int32(owned))


def first_kernel(senders, owned, state, rows, cols, source, blocks, *refs):
    slots, refs = refs[:senders], refs[senders:]
    kept, operand, pieces, made, op_sem, in_sem, slot_sem, keep_sem = refs
    place = state[0]
    stored, _ = blocks.shape[:2]
    batches, shots = source.shape[0], source.shape[-1]

    def load(block):
        return pltpu.make_async_copy(blocks.at[block], operand.at[block], op_sem.at[block])

    def fetch(block, batch):
        return pltpu.make_async_copy(
            source.at[batch, cols[block] - place * owned],
            pieces.at[block, :, pl.ds(batch * shots, shots)],
            in_sem.at[block, batch],
        )

    def give(block, slot):
        return pltpu.make_async_copy(made.at[block], slots[slot], slot_sem.at[block])

    def keep(block, owner):
        return pltpu.make_async_copy(made.at[block], kept.at[owner], keep_sem.at[block])

    @pl.loop(0, stored)
    def _(block):
        for batch in range(batches):
            fetch(block, batch).start()
        load(block).start()

    @pl.loop(0, stored)
    def _(block):
        for batch in range(batches):
            fetch(block, batch).wait()
        load(block).wait()
        product = jnp.dot(operand[block], pieces[block], preferred_element_type=jnp.float32)
        for batch in range(batches):
            made[block, batch] = product[:, batch * shots : (batch + 1) * shots].astype(made.dtype)
        owner = owner_of(rows[place, block], owned)
        shift = lax.rem(owner - place + senders, senders)
        for slot in range(senders):

            @pl.when(shift == slot)
            def _():
                give(block, slot).start()

        keep(block, owner).start()

    @pl.loop(0, stored)
    def _(block):
        give(block, 0).wait()
        keep(block, 0).wait()


def renew_kernel(senders, owned, state, rows, cols, match, go, source, blocks, *refs):
    recv, refs = refs[:senders], refs[senders:]
    kept, operand, pieces, arrived, total, made, op_sem, in_sem, recv_sem, keep_sem = refs[1:]
    place = state[0]
    stored, _ = blocks.shape[:2]
    batches, shots = source.shape[0], source.shape[-1]

    def load(block):
        return pltpu.make_async_copy(blocks.at[block], operand.at[block], op_sem.at[block])

    def fetch(block, batch):
        return pltpu.make_async_copy(
            source.at[batch, cols[block] - place * owned],
            pieces.at[block, :, pl.ds(batch * shots, shots)],
            in_sem.at[block, batch],
        )

    def take(step):
        return pltpu.make_async_copy(recv[step], arrived.at[step], recv_sem.at[step])

    def keep(block, owner):
        return pltpu.make_async_copy(made.at[block], kept.at[owner], keep_sem.at[block])

    def hits(block):
        return match[block, senders]

    def sender_at(step):
        return lax.rem(place - step + senders, senders)

    @pl.when(go[0] > 0)
    def _():
        for step in range(senders):

            @pl.when(match[stored, sender_at(step)] > 0)
            def _():
                take(step).start()

        @pl.loop(0, stored)
        def _(block):
            @pl.when(hits(block) > 0)
            def _():
                for batch in range(batches):
                    fetch(block, batch).start()
                load(block).start()

        for step in range(senders):

            @pl.when(match[stored, sender_at(step)] > 0)
            def _():
                take(step).wait()

        @pl.loop(0, stored)
        def _(block):
            @pl.when(hits(block) > 0)
            def _():
                total[...] = jnp.zeros_like(total)

                @pl.loop(0, senders)
                def _(step):
                    @pl.when(match[block, sender_at(step)] > 0)
                    def _():
                        total[...] += arrived[step].astype(jnp.float32)

                for batch in range(batches):
                    fetch(block, batch).wait()
                for batch in range(batches):
                    lanes = pl.ds(batch * shots, shots)
                    incoming = total[batch].astype(pieces.dtype).astype(jnp.float32)
                    pieces[block, :, lanes] = (
                        incoming + pieces[block, :, lanes].astype(jnp.float32)
                    ).astype(pieces.dtype)
                load(block).wait()
                product = jnp.dot(operand[block], pieces[block], preferred_element_type=jnp.float32)
                for batch in range(batches):
                    made[block, batch] = product[:, batch * shots : (batch + 1) * shots].astype(made.dtype)
                keep(block, owner_of(rows[place, block], owned)).start()

        @pl.loop(0, stored)
        def _(block):
            @pl.when(hits(block) > 0)
            def _():
                keep(block, 0).wait()


def hit_rows(rows, senders, place, owned, stored, here):
    first = place * owned

    @pl.loop(0, senders)
    def _(sender):
        row = jnp.int32(-1)
        for other in range(stored):
            value = rows[sender, other] - first
            row = jnp.where((value >= 0) & (value < owned), value, row)
        here[sender] = row


def zero_kernel(owned, senders, stored, batches, state, rows, after, out, nothing, here, sem):
    hit_rows(rows, senders, state[0], owned, stored, here)
    nothing[...] = jnp.zeros_like(nothing)

    def free(row):
        total = jnp.int32(0)
        for sender in range(senders):
            total += (here[sender] == row).astype(jnp.int32)
        return total == 0

    def put(batch, row):
        return pltpu.make_async_copy(nothing, out.at[batch, row], sem.at[batch, row])

    @pl.loop(0, owned)
    def _(row):
        @pl.when(free(row))
        def _():
            for batch in range(batches):
                put(batch, row).start()

    @pl.loop(0, owned)
    def _(row):
        @pl.when(free(row))
        def _():
            for batch in range(batches):
                put(batch, row).wait()


def write_kernel(owned, senders, stored, batches, state, rows, recv, old, out, arrived, total, made, here, in_sem, out_sem):
    hit_rows(rows, senders, state[0], owned, stored, here)

    def take(sender):
        return pltpu.make_async_copy(recv.at[sender], arrived.at[sender], in_sem.at[sender])

    def put(sender, batch, box):
        return pltpu.make_async_copy(box.at[sender, batch], out.at[batch, here[sender]], out_sem.at[sender, batch])

    def count(sender, first, last):
        total = jnp.int32(0)
        for other in range(senders):
            same = (here[other] == here[sender]) & (other >= first) & (other < last)
            total += same.astype(jnp.int32)
        return total

    @pl.loop(0, senders)
    def _(sender):
        @pl.when(here[sender] >= 0)
        def _():
            take(sender).start()

    @pl.loop(0, senders)
    def _(sender):
        @pl.when(here[sender] >= 0)
        def _():
            take(sender).wait()

    @pl.loop(0, senders)
    def _(sender):
        @pl.when((here[sender] >= 0) & (count(sender, 0, sender) == 0))
        def _():
            more = count(sender, sender + 1, senders)

            @pl.when(more == 0)
            def _():
                for batch in range(batches):
                    put(sender, batch, arrived).start()

            @pl.when(more > 0)
            def _():
                total[...] = arrived[sender].astype(jnp.float32)

                @pl.loop(sender + 1, senders)
                def _(other):
                    @pl.when(here[other] == here[sender])
                    def _():
                        total[...] += arrived[other].astype(jnp.float32)

                made[sender] = total[...].astype(made.dtype)
                for batch in range(batches):
                    put(sender, batch, made).start()

    @pl.loop(0, senders)
    def _(sender):
        @pl.when((here[sender] >= 0) & (count(sender, 0, sender) == 0))
        def _():
            for batch in range(batches):
                put(sender, batch, made).wait()


def body(operators, sources, row_block, col_block):
    place = lax.axis_index("trace")
    depth = lax.axis_index("layer")
    senders = lax.axis_size("trace")
    layers = lax.axis_size("layer")
    blocks = operators[0]
    rows = row_block[0]
    stored, width = blocks.shape[0], blocks.shape[-1]
    batches, local, shots = sources.shape[1:]
    owned = local // width
    source = sources.reshape(batches, owned, width, shots)
    cols = col_block[0, 0]
    state = jnp.stack([place, depth]).astype(jnp.int32)
    dtype = sources.dtype
    tile = (batches, width, shots)
    slot = jax.ShapeDtypeStruct(tile, dtype)
    held = jax.ShapeDtypeStruct((senders,) + tile, dtype)

    def pairs(step):
        return [
            (i * senders + j, (i + 1) * senders + (j + step) % senders)
            for i in range(layers - 1)
            for j in range(senders)
        ]

    *slots, kept = pl.pallas_call(
        lambda *refs: first_kernel(senders, owned, *refs),
        out_shape=(slot,) * senders + (held,),
        in_specs=[SMEM] * 3 + [ANY] * 2,
        out_specs=(ANY,) * (senders + 1),
        scratch_shapes=[
            pltpu.VMEM((stored, width, width), dtype),
            pltpu.VMEM((stored, width, batches * shots), dtype),
            pltpu.VMEM((stored,) + tile, dtype),
            DMA((stored,)),
            DMA((stored, batches)),
            DMA((stored,)),
            DMA((stored,)),
        ],
        compiler_params=PARAMS,
        name="first",
    )(state, rows, cols, source, blocks)
    recv = []
    for step in range(senders):
        recv.append(lax.ppermute(slots[step], AXES, pairs(step)))

    total = layers * senders
    mine = jnp.concatenate([rows.reshape(-1), cols])
    mine, kept = lax.optimization_barrier((mine, kept))
    mine = jnp.broadcast_to(mine[None], (total, mine.shape[0]))
    known = lax.all_to_all(mine, AXES, split_axis=0, concat_axis=0, tiled=True)
    known = known.reshape(layers, senders, -1)
    blocks_all = senders * stored
    rows_all = known[:, 0, :blocks_all]
    cols_all = known[:, :, blocks_all:].reshape(layers, blocks_all)
    feeds = rows_all[:-1, :, None] == cols_all[1:, None, :]
    read = jnp.any(feeds, axis=2)
    home = jnp.repeat(jnp.arange(senders, dtype=jnp.int32), stored)
    shift = (rows_all[:-1] // owned - home[None, :]) % senders
    steps = jnp.arange(senders, dtype=jnp.int32)
    changed = jnp.any(feeds, axis=1)
    masks = []
    group = 4 if senders <= 8 else 2
    for _ in range(2, layers):
        below = jnp.concatenate([jnp.zeros((1, blocks_all), bool), changed[:-1]])
        again = below & read
        mask = jnp.any(again[:, :, None] & (shift[:, :, None] == steps), axis=(0, 1)).astype(jnp.int32)
        masks.append(mask)
        changed = jnp.any(feeds & below[:, :, None], axis=1)

    above = lax.dynamic_index_in_dim(rows_all, jnp.maximum(depth - 1, 0), 0, keepdims=False)
    above = above.reshape(senders, stored)
    match = jnp.any((above[None] == cols[:, None, None]) & (depth > 0), axis=2).astype(jnp.int32)
    match = jnp.concatenate([match, jnp.max(match, axis=0, keepdims=True)])
    match = jnp.concatenate([match, jnp.max(match, axis=1, keepdims=True)], axis=1)

    def renew(kept, go):
        return pl.pallas_call(
            lambda *refs: renew_kernel(senders, owned, *refs),
            out_shape=held,
            in_specs=[SMEM] * 5 + [ANY] * (3 + senders),
            out_specs=ANY,
            scratch_shapes=[
                pltpu.VMEM((stored, width, width), dtype),
                pltpu.VMEM((stored, width, batches * shots), dtype),
                pltpu.VMEM((senders,) + tile, dtype),
                pltpu.VMEM(tile, jnp.float32),
                pltpu.VMEM((stored,) + tile, dtype),
                DMA((stored,)),
                DMA((stored, batches)),
                DMA((senders,)),
                DMA((stored,)),
            ],
            input_output_aliases={7 + senders: 0},
            compiler_params=PARAMS,
            name="renew",
        )(state, rows, cols, match, go[None], source, blocks, *recv, kept)

    traces = pl.pallas_call(
        lambda *refs: zero_kernel(owned, senders, stored, batches, *refs),
        out_shape=jax.ShapeDtypeStruct((batches, owned, width, shots), dtype),
        in_specs=[SMEM, SMEM, ANY],
        out_specs=ANY,
        scratch_shapes=[
            pltpu.VMEM((width, shots), dtype),
            pltpu.SMEM((senders,), jnp.int32),
            DMA((batches, owned)),
        ],
        compiler_params=PARAMS,
        name="zeros",
    )(state, rows, recv[0])

    kept = renew(kept, jnp.int32(1))

    def again(step, kept):
        sent = lax.dynamic_index_in_dim(kept, (place + step) % senders, 0, keepdims=False)
        return lax.ppermute(sent, AXES, pairs(step))

    for wave, mask in enumerate(masks):
        if wave == 0:
            for low in range(0, senders, group):
                near = range(low, min(low + group, senders))

                def resend(which):
                    return lambda kept, old: tuple(
                        again(step, kept) if which >> at & 1 else old[at] for at, step in enumerate(near)
                    )

                code = sum(mask[step] << at for at, step in enumerate(near))
                recv[low : low + group] = lax.switch(
                    code, [resend(which) for which in range(1 << len(near))], kept, tuple(recv[low : low + group])
                )
        else:

            def resend_one(carry):
                left, mask, recv = carry
                step = jnp.argmax(mask).astype(jnp.int32)
                recv = lax.switch(
                    step,
                    [
                        lambda kept, recv, step=step: recv[:step] + (again(step, kept),) + recv[step + 1 :]
                        for step in range(senders)
                    ],
                    kept,
                    recv,
                )
                return left - 1, jnp.where(steps == step, 0, mask), recv

            recv = list(lax.while_loop(lambda carry: carry[0] > 0, resend_one, (jnp.sum(mask), mask, tuple(recv)))[2])
        kept = renew(kept, jnp.max(mask))

    arrived = lax.all_to_all(kept, "trace", split_axis=0, concat_axis=0, tiled=True)
    traces = pl.pallas_call(
        lambda *refs: write_kernel(owned, senders, stored, batches, *refs),
        out_shape=jax.ShapeDtypeStruct((batches, owned, width, shots), dtype),
        in_specs=[SMEM, SMEM, ANY, ANY],
        out_specs=ANY,
        scratch_shapes=[
            pltpu.VMEM((senders,) + tile, dtype),
            pltpu.VMEM(tile, jnp.float32),
            pltpu.VMEM((senders,) + tile, dtype),
            pltpu.SMEM((senders,), jnp.int32),
            DMA((senders,)),
            DMA((senders, batches)),
        ],
        input_output_aliases={3: 0},
        compiler_params=PARAMS,
        name="write",
    )(state, rows, arrived, traces)
    return traces.reshape(1, batches, local, shots)


def solution(mesh):
    placed = (
        P("layer", "trace", None, None),
        P("layer", None, "trace", None),
        P("layer", None, None),
        P("layer", "trace", None),
    )
    return jax.shard_map(
        body, mesh=mesh, in_specs=placed, out_specs=P("layer", None, "trace", None), check_vma=False
    )
```

```python
import jax
import jax.numpy as jnp
from jax import lax
from jax.experimental import pallas as pl
from jax.experimental.pallas import tpu as pltpu
from jax.sharding import PartitionSpec as P


AXES = ("layer", "trace")
SMEM = pl.BlockSpec(memory_space=pltpu.SMEM)
ANY = pl.BlockSpec(memory_space=pl.ANY)
PARAMS = pltpu.CompilerParams(vmem_limit_bytes=67043328)
DMA = pltpu.SemaphoreType.DMA


def owner_of(row, owned):
    if owned & (owned - 1) == 0:
        return lax.shift_right_logical(row, jnp.int32(owned.bit_length() - 1))
    return lax.div(row, jnp.int32(owned))


def first_kernel(senders, owned, state, rows, cols, source, blocks, *refs):
    slots, refs = refs[:senders], refs[senders:]
    kept, operand, pieces, made, op_sem, in_sem, slot_sem, keep_sem = refs
    place = state[0]
    stored, _ = blocks.shape[:2]
    batches, shots = source.shape[0], source.shape[-1]

    def load(block):
        return pltpu.make_async_copy(blocks.at[block], operand.at[block], op_sem.at[block])

    def fetch(block, batch):
        return pltpu.make_async_copy(
            source.at[batch, cols[block] - place * owned],
            pieces.at[block, :, pl.ds(batch * shots, shots)],
            in_sem.at[block, batch],
        )

    def give(block, slot):
        return pltpu.make_async_copy(made.at[block], slots[slot], slot_sem.at[block])

    def keep(block, owner):
        return pltpu.make_async_copy(made.at[block], kept.at[owner], keep_sem.at[block])

    @pl.loop(0, stored)
    def _(block):
        for batch in range(batches):
            fetch(block, batch).start()
        load(block).start()

    @pl.loop(0, stored)
    def _(block):
        for batch in range(batches):
            fetch(block, batch).wait()
        load(block).wait()
        product = jnp.dot(operand[block], pieces[block], preferred_element_type=jnp.float32)
        for batch in range(batches):
            made[block, batch] = product[:, batch * shots : (batch + 1) * shots].astype(made.dtype)
        owner = owner_of(rows[place, block], owned)
        shift = lax.rem(owner - place + senders, senders)
        for slot in range(senders):

            @pl.when(shift == slot)
            def _():
                give(block, slot).start()

        keep(block, owner).start()

    @pl.loop(0, stored)
    def _(block):
        give(block, 0).wait()
        keep(block, 0).wait()


def renew_kernel(senders, owned, state, rows, cols, match, go, source, blocks, *refs):
    recv, refs = refs[:senders], refs[senders:]
    kept, operand, pieces, arrived, total, made, op_sem, in_sem, recv_sem, keep_sem = refs[1:]
    place = state[0]
    stored, _ = blocks.shape[:2]
    batches, shots = source.shape[0], source.shape[-1]

    def load(block):
        return pltpu.make_async_copy(blocks.at[block], operand.at[block], op_sem.at[block])

    def fetch(block, batch):
        return pltpu.make_async_copy(
            source.at[batch, cols[block] - place * owned],
            pieces.at[block, :, pl.ds(batch * shots, shots)],
            in_sem.at[block, batch],
        )

    def take(step):
        return pltpu.make_async_copy(recv[step], arrived.at[step], recv_sem.at[step])

    def keep(block, owner):
        return pltpu.make_async_copy(made.at[block], kept.at[owner], keep_sem.at[block])

    def hits(block):
        return match[block, senders]

    def sender_at(step):
        return lax.rem(place - step + senders, senders)

    @pl.when(go[0] > 0)
    def _():
        for step in range(senders):

            @pl.when(match[stored, sender_at(step)] > 0)
            def _():
                take(step).start()

        @pl.loop(0, stored)
        def _(block):
            @pl.when(hits(block) > 0)
            def _():
                for batch in range(batches):
                    fetch(block, batch).start()
                load(block).start()

        for step in range(senders):

            @pl.when(match[stored, sender_at(step)] > 0)
            def _():
                take(step).wait()

        @pl.loop(0, stored)
        def _(block):
            @pl.when(hits(block) > 0)
            def _():
                total[...] = jnp.zeros_like(total)

                @pl.loop(0, senders)
                def _(step):
                    @pl.when(match[block, sender_at(step)] > 0)
                    def _():
                        total[...] += arrived[step].astype(jnp.float32)

                for batch in range(batches):
                    fetch(block, batch).wait()
                for batch in range(batches):
                    lanes = pl.ds(batch * shots, shots)
                    incoming = total[batch].astype(pieces.dtype).astype(jnp.float32)
                    pieces[block, :, lanes] = (
                        incoming + pieces[block, :, lanes].astype(jnp.float32)
                    ).astype(pieces.dtype)
                load(block).wait()
                product = jnp.dot(operand[block], pieces[block], preferred_element_type=jnp.float32)
                for batch in range(batches):
                    made[block, batch] = product[:, batch * shots : (batch + 1) * shots].astype(made.dtype)
                keep(block, owner_of(rows[place, block], owned)).start()

        @pl.loop(0, stored)
        def _(block):
            @pl.when(hits(block) > 0)
            def _():
                keep(block, 0).wait()


def hit_rows(rows, senders, place, owned, stored, here):
    first = place * owned

    @pl.loop(0, senders)
    def _(sender):
        row = jnp.int32(-1)
        for other in range(stored):
            value = rows[sender, other] - first
            row = jnp.where((value >= 0) & (value < owned), value, row)
        here[sender] = row


def zero_kernel(owned, senders, stored, batches, state, rows, after, out, nothing, here, sem):
    hit_rows(rows, senders, state[0], owned, stored, here)
    nothing[...] = jnp.zeros_like(nothing)

    def free(row):
        total = jnp.int32(0)
        for sender in range(senders):
            total += (here[sender] == row).astype(jnp.int32)
        return total == 0

    def put(batch, row):
        return pltpu.make_async_copy(nothing, out.at[batch, row], sem.at[batch, row])

    @pl.loop(0, owned)
    def _(row):
        @pl.when(free(row))
        def _():
            for batch in range(batches):
                put(batch, row).start()

    @pl.loop(0, owned)
    def _(row):
        @pl.when(free(row))
        def _():
            for batch in range(batches):
                put(batch, row).wait()


def write_kernel(owned, senders, stored, batches, state, rows, fixed, recv, *refs):
    fixes, refs = refs[:senders], refs[senders:]
    _, out, arrived, total, made, here, in_sem, out_sem = refs
    hit_rows(rows, senders, state[0], owned, stored, here)

    def take(sender):
        return pltpu.make_async_copy(recv.at[sender], arrived.at[sender], in_sem.at[sender])

    def put(sender, batch, box):
        return pltpu.make_async_copy(box.at[sender, batch], out.at[batch, here[sender]], out_sem.at[sender, batch])

    def count(sender, first, last):
        total = jnp.int32(0)
        for other in range(senders):
            same = (here[other] == here[sender]) & (other >= first) & (other < last)
            total += same.astype(jnp.int32)
        return total

    for step in range(senders):
        sender = lax.rem(state[0] - step + senders, senders)

        @pl.when((here[sender] >= 0) & (fixed[sender] == 0))
        def _():
            take(sender).start()

        @pl.when((here[sender] >= 0) & (fixed[sender] > 0))
        def _():
            pltpu.make_async_copy(fixes[step], arrived.at[sender], in_sem.at[sender]).start()

    @pl.loop(0, senders)
    def _(sender):
        @pl.when(here[sender] >= 0)
        def _():
            take(sender).wait()

    @pl.loop(0, senders)
    def _(sender):
        @pl.when((here[sender] >= 0) & (count(sender, 0, sender) == 0))
        def _():
            more = count(sender, sender + 1, senders)

            @pl.when(more == 0)
            def _():
                for batch in range(batches):
                    put(sender, batch, arrived).start()

            @pl.when(more > 0)
            def _():
                total[...] = arrived[sender].astype(jnp.float32)

                @pl.loop(sender + 1, senders)
                def _(other):
                    @pl.when(here[other] == here[sender])
                    def _():
                        total[...] += arrived[other].astype(jnp.float32)

                made[sender] = total[...].astype(made.dtype)
                for batch in range(batches):
                    put(sender, batch, made).start()

    @pl.loop(0, senders)
    def _(sender):
        @pl.when((here[sender] >= 0) & (count(sender, 0, sender) == 0))
        def _():
            for batch in range(batches):
                put(sender, batch, made).wait()


def body(operators, sources, row_block, col_block):
    place = lax.axis_index("trace")
    depth = lax.axis_index("layer")
    senders = lax.axis_size("trace")
    layers = lax.axis_size("layer")
    blocks = operators[0]
    rows = row_block[0]
    stored, width = blocks.shape[0], blocks.shape[-1]
    batches, local, shots = sources.shape[1:]
    owned = local // width
    source = sources.reshape(batches, owned, width, shots)
    cols = col_block[0, 0]
    state = jnp.stack([place, depth]).astype(jnp.int32)
    dtype = sources.dtype
    tile = (batches, width, shots)
    slot = jax.ShapeDtypeStruct(tile, dtype)
    held = jax.ShapeDtypeStruct((senders,) + tile, dtype)

    def pairs(step, down=1):
        return [
            (i * senders + j, (i + down) * senders + (j + step) % senders)
            for i in range(layers - down)
            for j in range(senders)
        ]

    *slots, kept = pl.pallas_call(
        lambda *refs: first_kernel(senders, owned, *refs),
        out_shape=(slot,) * senders + (held,),
        in_specs=[SMEM] * 3 + [ANY] * 2,
        out_specs=(ANY,) * (senders + 1),
        scratch_shapes=[
            pltpu.VMEM((stored, width, width), dtype),
            pltpu.VMEM((stored, width, batches * shots), dtype),
            pltpu.VMEM((stored,) + tile, dtype),
            DMA((stored,)),
            DMA((stored, batches)),
            DMA((stored,)),
            DMA((stored,)),
        ],
        compiler_params=PARAMS,
        name="first",
    )(state, rows, cols, source, blocks)
    recv = []
    for step in range(senders):
        recv.append(lax.ppermute(slots[step], AXES, pairs(step)))

    total = layers * senders
    mine = jnp.concatenate([rows.reshape(-1), cols])
    mine, kept = lax.optimization_barrier((mine, kept))
    mine = jnp.broadcast_to(mine[None], (total, mine.shape[0]))
    known = lax.all_to_all(mine, AXES, split_axis=0, concat_axis=0, tiled=True)
    known = known.reshape(layers, senders, -1)
    blocks_all = senders * stored
    rows_all = known[:, 0, :blocks_all]
    cols_all = known[:, :, blocks_all:].reshape(layers, blocks_all)
    feeds = rows_all[:-1, :, None] == cols_all[1:, None, :]
    read = jnp.any(feeds, axis=2)
    home = jnp.repeat(jnp.arange(senders, dtype=jnp.int32), stored)
    shift_all = (rows_all // owned - home[None, :]) % senders
    shift = shift_all[:-1]
    steps = jnp.arange(senders, dtype=jnp.int32)
    changed = jnp.any(feeds, axis=1)
    later = jnp.zeros(changed.shape, bool)
    masks = []
    group = 4 if senders <= 8 else 2
    for wave in range(2, layers):
        below = jnp.concatenate([jnp.zeros((1, blocks_all), bool), changed[:-1]])
        again = below & read
        mask = jnp.any(again[:, :, None] & (shift[:, :, None] == steps), axis=(0, 1)).astype(jnp.int32)
        masks.append(mask)
        changed = jnp.any(feeds & below[:, :, None], axis=1)
        if wave > 2:
            later |= changed
    late_mask = jnp.any(later[:, :, None] & (shift_all[1:, :, None] == steps), axis=(0, 1)).astype(jnp.int32)
    mine_later = lax.dynamic_index_in_dim(later, jnp.maximum(depth - 1, 0), 0, keepdims=False) & (depth > 0)
    to_me = (rows // owned == place).reshape(-1) & mine_later
    fixed = jnp.any(to_me.reshape(senders, stored), axis=1).astype(jnp.int32)

    above = lax.dynamic_index_in_dim(rows_all, jnp.maximum(depth - 1, 0), 0, keepdims=False)
    above = above.reshape(senders, stored)
    match = jnp.any((above[None] == cols[:, None, None]) & (depth > 0), axis=2).astype(jnp.int32)
    match = jnp.concatenate([match, jnp.max(match, axis=0, keepdims=True)])
    match = jnp.concatenate([match, jnp.max(match, axis=1, keepdims=True)], axis=1)

    def renew(kept, go):
        return pl.pallas_call(
            lambda *refs: renew_kernel(senders, owned, *refs),
            out_shape=held,
            in_specs=[SMEM] * 5 + [ANY] * (3 + senders),
            out_specs=ANY,
            scratch_shapes=[
                pltpu.VMEM((stored, width, width), dtype),
                pltpu.VMEM((stored, width, batches * shots), dtype),
                pltpu.VMEM((senders,) + tile, dtype),
                pltpu.VMEM(tile, jnp.float32),
                pltpu.VMEM((stored,) + tile, dtype),
                DMA((stored,)),
                DMA((stored, batches)),
                DMA((senders,)),
                DMA((stored,)),
            ],
            input_output_aliases={7 + senders: 0},
            compiler_params=PARAMS,
            name="renew",
        )(state, rows, cols, match, go[None], source, blocks, *recv, kept)

    traces = pl.pallas_call(
        lambda *refs: zero_kernel(owned, senders, stored, batches, *refs),
        out_shape=jax.ShapeDtypeStruct((batches, owned, width, shots), dtype),
        in_specs=[SMEM, SMEM, ANY],
        out_specs=ANY,
        scratch_shapes=[
            pltpu.VMEM((width, shots), dtype),
            pltpu.SMEM((senders,), jnp.int32),
            DMA((batches, owned)),
        ],
        compiler_params=PARAMS,
        name="zeros",
    )(state, rows, recv[0])

    kept = renew(kept, jnp.int32(1))

    def again(step, kept, down=1):
        sent = lax.dynamic_index_in_dim(kept, (place + step) % senders, 0, keepdims=False)
        return lax.ppermute(sent, AXES, pairs(step, down))

    def one_by_one(mask, send, came):
        def resend(carry):
            left, mask, came = carry
            step = jnp.argmax(mask).astype(jnp.int32)
            branches = [
                lambda came, step=step: came[:step] + (send(step),) + came[step + 1 :] for step in range(senders)
            ]
            return left - 1, jnp.where(steps == step, 0, mask), lax.switch(step, branches, came)

        return lax.while_loop(lambda carry: carry[0] > 0, resend, (jnp.sum(mask), mask, tuple(came)))[2]

    if masks:
        for low in range(0, senders, group):
            near = range(low, min(low + group, senders))

            def resend(which):
                return lambda kept, old: tuple(
                    again(step, kept) if which >> at & 1 else old[at] for at, step in enumerate(near)
                )

            code = sum(masks[0][step] << at for at, step in enumerate(near))
            recv[low : low + group] = lax.switch(
                code, [resend(which) for which in range(1 << len(near))], kept, tuple(recv[low : low + group])
            )
        kept = renew(kept, jnp.max(masks[0]))
    arrived = lax.all_to_all(kept, "trace", split_axis=0, concat_axis=0, tiled=True)

    late = kept
    for mask in masks[1:]:
        recv = list(one_by_one(mask, lambda step, late=late: again(step, late), recv))
        late = renew(late, jnp.max(mask))
    fixes = one_by_one(late_mask, lambda step: again(step, late, 0), recv)

    traces = pl.pallas_call(
        lambda *refs: write_kernel(owned, senders, stored, batches, *refs),
        out_shape=jax.ShapeDtypeStruct((batches, owned, width, shots), dtype),
        in_specs=[SMEM] * 3 + [ANY] * (senders + 2),
        out_specs=ANY,
        scratch_shapes=[
            pltpu.VMEM((senders,) + tile, dtype),
            pltpu.VMEM(tile, jnp.float32),
            pltpu.VMEM((senders,) + tile, dtype),
            pltpu.SMEM((senders,), jnp.int32),
            DMA((senders,)),
            DMA((senders, batches)),
        ],
        input_output_aliases={4 + senders: 0},
        compiler_params=PARAMS,
        name="write",
    )(state, rows, fixed, arrived, *fixes, traces)
    return traces.reshape(1, batches, local, shots)


def solution(mesh):
    placed = (
        P("layer", "trace", None, None),
        P("layer", None, "trace", None),
        P("layer", None, None),
        P("layer", "trace", None),
    )
    return jax.shard_map(
        body, mesh=mesh, in_specs=placed, out_specs=P("layer", None, "trace", None), check_vma=False
    )
```

```python
import jax
import jax.numpy as jnp
from jax import lax
from jax.experimental import pallas as pl
from jax.experimental.pallas import tpu as pltpu
from jax.sharding import PartitionSpec as P


AXES = ("layer", "trace")
SMEM = pl.BlockSpec(memory_space=pltpu.SMEM)
ANY = pl.BlockSpec(memory_space=pl.ANY)
PARAMS = pltpu.CompilerParams(vmem_limit_bytes=67043328)
DMA = pltpu.SemaphoreType.DMA


def owner_of(row, owned):
    if owned & (owned - 1) == 0:
        return lax.shift_right_logical(row, jnp.int32(owned.bit_length() - 1))
    return lax.div(row, jnp.int32(owned))


def read_table(table, senders, stored):
    held = senders * stored

    def rows(sender, block):
        return table[sender * stored + block]

    def cols(block):
        return table[held + block]

    def more(at):
        return table[held + stored + 1 + at]

    return rows, cols, table[held + stored], more


def first_kernel(senders, owned, rows_ref, cols_ref, source, blocks, *refs):
    slots, refs = refs[:senders], refs[senders:]
    kept, operand, pieces, made, op_sem, in_sem, slot_sem, keep_sem = refs
    stored, _ = blocks.shape[:2]
    place = lax.axis_index("trace")
    batches, shots = source.shape[0], source.shape[-1]

    def rows(sender, block):
        return rows_ref[0, sender, block]

    def load(block):
        return pltpu.make_async_copy(blocks.at[block], operand.at[block], op_sem.at[block])

    def fetch(block, batch):
        return pltpu.make_async_copy(
            source.at[batch, cols_ref[0, 0, block] - place * owned],
            pieces.at[block, :, pl.ds(batch * shots, shots)],
            in_sem.at[block, batch],
        )

    def give(block, slot):
        return pltpu.make_async_copy(made.at[block], slots[slot], slot_sem.at[block])

    def keep(block, owner):
        return pltpu.make_async_copy(made.at[block], kept.at[owner], keep_sem.at[block])

    @pl.loop(0, stored)
    def _(block):
        for batch in range(batches):
            fetch(block, batch).start()
        load(block).start()

    @pl.loop(0, stored)
    def _(block):
        for batch in range(batches):
            fetch(block, batch).wait()
        load(block).wait()
        product = jnp.dot(operand[block], pieces[block], preferred_element_type=jnp.float32)
        for batch in range(batches):
            made[block, batch] = product[:, batch * shots : (batch + 1) * shots].astype(made.dtype)
        owner = owner_of(rows(place, block), owned)
        shift = lax.rem(owner - place + senders, senders)
        for slot in range(senders):

            @pl.when(shift == slot)
            def _():
                give(block, slot).start()

        keep(block, owner).start()

    @pl.loop(0, stored)
    def _(block):
        give(block, 0).wait()
        keep(block, 0).wait()


def renew_kernel(senders, owned, others, resent, table, source, blocks, *refs):
    recv, refs = refs[:senders], refs[senders + 1 + resent + others :]
    slots, refs = refs[:resent], refs[resent:]
    kept, operand, pieces, arrived, total, made, op_sem, in_sem, recv_sem, keep_sem, slot_sem = refs
    stored, _ = blocks.shape[:2]
    rows, cols, place, more = read_table(table, senders, stored)
    go = more(0) > 0

    def match(block, sender):
        return more(1 + block * (senders + 1) + sender)

    batches, shots = source.shape[0], source.shape[-1]

    def load(block):
        return pltpu.make_async_copy(blocks.at[block], operand.at[block], op_sem.at[block])

    def fetch(block, batch):
        return pltpu.make_async_copy(
            source.at[batch, cols(block) - place * owned],
            pieces.at[block, :, pl.ds(batch * shots, shots)],
            in_sem.at[block, batch],
        )

    def take(step):
        return pltpu.make_async_copy(recv[step], arrived.at[step], recv_sem.at[step])

    def keep(block, owner):
        return pltpu.make_async_copy(made.at[block], kept.at[owner], keep_sem.at[block])

    def give(block, slot):
        return pltpu.make_async_copy(made.at[block], slots[slot], slot_sem.at[block])

    def hits(block):
        return match(block, senders)

    def sender_at(step):
        return lax.rem(place - step + senders, senders)

    @pl.when(go)
    def _():
        for step in range(senders):

            @pl.when(match(stored, sender_at(step)) > 0)
            def _():
                take(step).start()

        @pl.loop(0, stored)
        def _(block):
            @pl.when(hits(block) > 0)
            def _():
                for batch in range(batches):
                    fetch(block, batch).start()
                load(block).start()

        for step in range(senders):

            @pl.when(match(stored, sender_at(step)) > 0)
            def _():
                take(step).wait()

        @pl.loop(0, stored)
        def _(block):
            @pl.when(hits(block) > 0)
            def _():
                total[...] = jnp.zeros_like(total)

                @pl.loop(0, senders)
                def _(step):
                    @pl.when(match(block, sender_at(step)) > 0)
                    def _():
                        total[...] += arrived[step].astype(jnp.float32)

                for batch in range(batches):
                    fetch(block, batch).wait()
                for batch in range(batches):
                    lanes = pl.ds(batch * shots, shots)
                    incoming = total[batch].astype(pieces.dtype).astype(jnp.float32)
                    pieces[block, :, lanes] = (
                        incoming + pieces[block, :, lanes].astype(jnp.float32)
                    ).astype(pieces.dtype)
                load(block).wait()
                product = jnp.dot(operand[block], pieces[block], preferred_element_type=jnp.float32)
                for batch in range(batches):
                    made[block, batch] = product[:, batch * shots : (batch + 1) * shots].astype(made.dtype)
                owner = owner_of(rows(place, block), owned)
                keep(block, owner).start()
                for slot in range(resent):

                    @pl.when(lax.rem(owner - place + senders, senders) == slot)
                    def _():
                        give(block, slot).start()

        @pl.loop(0, stored)
        def _(block):
            @pl.when(hits(block) > 0)
            def _():
                keep(block, 0).wait()
                if resent:
                    give(block, 0).wait()


def hit_rows(rows, senders, place, owned, stored, here):
    first = place * owned

    @pl.loop(0, senders)
    def _(sender):
        row = jnp.int32(-1)
        for other in range(stored):
            value = rows(sender, other) - first
            row = jnp.where((value >= 0) & (value < owned), value, row)
        here[sender] = row


def zero_kernel(owned, senders, stored, batches, table, after, out, nothing, here, sem):
    rows, _, place, _ = read_table(table, senders, stored)
    hit_rows(rows, senders, place, owned, stored, here)
    nothing[...] = jnp.zeros_like(nothing)

    def free(row):
        total = jnp.int32(0)
        for sender in range(senders):
            total += (here[sender] == row).astype(jnp.int32)
        return total == 0

    def put(batch, row):
        return pltpu.make_async_copy(nothing, out.at[batch, row], sem.at[batch, row])

    @pl.loop(0, owned)
    def _(row):
        @pl.when(free(row))
        def _():
            for batch in range(batches):
                put(batch, row).start()

    @pl.loop(0, owned)
    def _(row):
        @pl.when(free(row))
        def _():
            for batch in range(batches):
                put(batch, row).wait()


def write_kernel(owned, senders, stored, batches, table, recv, *refs):
    fixes, refs = refs[:senders], refs[senders:]
    _, out, arrived, total, made, here, in_sem, out_sem = refs
    rows, _, place, fixed = read_table(table, senders, stored)
    hit_rows(rows, senders, place, owned, stored, here)

    def take(sender):
        return pltpu.make_async_copy(recv.at[sender], arrived.at[sender], in_sem.at[sender])

    def put(sender, batch, box):
        return pltpu.make_async_copy(box.at[sender, batch], out.at[batch, here[sender]], out_sem.at[sender, batch])

    def count(sender, first, last):
        total = jnp.int32(0)
        for other in range(senders):
            same = (here[other] == here[sender]) & (other >= first) & (other < last)
            total += same.astype(jnp.int32)
        return total

    for step in range(senders):
        sender = lax.rem(place - step + senders, senders)

        @pl.when((here[sender] >= 0) & (fixed(sender) == 0))
        def _():
            take(sender).start()

        @pl.when((here[sender] >= 0) & (fixed(sender) > 0))
        def _():
            pltpu.make_async_copy(fixes[step], arrived.at[sender], in_sem.at[sender]).start()

    @pl.loop(0, senders)
    def _(sender):
        @pl.when(here[sender] >= 0)
        def _():
            take(sender).wait()

    @pl.loop(0, senders)
    def _(sender):
        @pl.when((here[sender] >= 0) & (count(sender, 0, sender) == 0))
        def _():
            more = count(sender, sender + 1, senders)

            @pl.when(more == 0)
            def _():
                for batch in range(batches):
                    put(sender, batch, arrived).start()

            @pl.when(more > 0)
            def _():
                total[...] = arrived[sender].astype(jnp.float32)

                @pl.loop(sender + 1, senders)
                def _(other):
                    @pl.when(here[other] == here[sender])
                    def _():
                        total[...] += arrived[other].astype(jnp.float32)

                made[sender] = total[...].astype(made.dtype)
                for batch in range(batches):
                    put(sender, batch, made).start()

    @pl.loop(0, senders)
    def _(sender):
        @pl.when((here[sender] >= 0) & (count(sender, 0, sender) == 0))
        def _():
            for batch in range(batches):
                put(sender, batch, made).wait()


def body(operators, sources, row_block, col_block):
    place = lax.axis_index("trace")
    depth = lax.axis_index("layer")
    senders = lax.axis_size("trace")
    layers = lax.axis_size("layer")
    blocks = operators[0]
    rows = row_block[0]
    stored, width = blocks.shape[0], blocks.shape[-1]
    batches, local, shots = sources.shape[1:]
    owned = local // width
    source = sources.reshape(batches, owned, width, shots)
    cols = col_block[0, 0]
    table = jnp.concatenate([rows.reshape(-1), cols, place[None].astype(jnp.int32)])
    dtype = sources.dtype
    tile = (batches, width, shots)
    slot = jax.ShapeDtypeStruct(tile, dtype)
    held = jax.ShapeDtypeStruct((senders,) + tile, dtype)

    def pairs(step, down=1, top=0):
        return [
            (i * senders + j, (i + down) * senders + (j + step) % senders)
            for i in range(top, layers - down)
            for j in range(senders)
        ]

    *slots, kept = pl.pallas_call(
        lambda *refs: first_kernel(senders, owned, *refs),
        out_shape=(slot,) * senders + (held,),
        in_specs=[SMEM] * 2 + [ANY] * 2,
        out_specs=(ANY,) * (senders + 1),
        scratch_shapes=[
            pltpu.VMEM((stored, width, width), dtype),
            pltpu.VMEM((stored, width, batches * shots), dtype),
            pltpu.VMEM((stored,) + tile, dtype),
            DMA((stored,)),
            DMA((stored, batches)),
            DMA((stored,)),
            DMA((stored,)),
        ],
        compiler_params=PARAMS,
        name="first",
    )(row_block, col_block, source, blocks)
    recv = [None] * senders
    for step in sorted(range(senders), key=lambda step: abs(2 * step - senders)):
        recv[step] = lax.ppermute(slots[step], AXES, pairs(step))

    total = layers * senders
    mine, kept = lax.optimization_barrier((table, kept))
    mine = jnp.broadcast_to(mine[None], (total, mine.shape[0]))
    known = lax.all_to_all(mine, AXES, split_axis=0, concat_axis=0, tiled=True)
    known = known.reshape(layers, senders, -1)
    blocks_all = senders * stored
    rows_all = known[:, 0, :blocks_all]
    cols_all = known[:, :, blocks_all : blocks_all + stored].reshape(layers, blocks_all)
    feeds = rows_all[:-1, :, None] == cols_all[1:, None, :]
    read = jnp.any(feeds, axis=2)
    home = jnp.repeat(jnp.arange(senders, dtype=jnp.int32), stored)
    shift_all = (rows_all // owned - home[None, :]) % senders
    shift = shift_all[:-1]
    steps = jnp.arange(senders, dtype=jnp.int32)
    changed = jnp.any(feeds, axis=1)
    later = jnp.zeros(changed.shape, bool)
    masks = []
    group = 4 if senders <= 8 else 2
    for wave in range(2, layers):
        below = jnp.concatenate([jnp.zeros((1, blocks_all), bool), changed[:-1]])
        again = below & read
        mask = jnp.any(again[:, :, None] & (shift[:, :, None] == steps), axis=(0, 1)).astype(jnp.int32)
        masks.append(mask)
        changed = jnp.any(feeds & below[:, :, None], axis=1)
        if wave > 2:
            later |= changed
    late_mask = jnp.any(later[:, :, None] & (shift_all[1:, :, None] == steps), axis=(0, 1)).astype(jnp.int32)
    mine_later = lax.dynamic_index_in_dim(later, jnp.maximum(depth - 1, 0), 0, keepdims=False) & (depth > 0)
    to_me = (rows // owned == place).reshape(-1) & mine_later
    fixed = jnp.any(to_me.reshape(senders, stored), axis=1).astype(jnp.int32)

    above = lax.dynamic_index_in_dim(rows_all, jnp.maximum(depth - 1, 0), 0, keepdims=False)
    above = above.reshape(senders, stored)
    match = jnp.any((above[None] == cols[:, None, None]) & (depth > 0), axis=2).astype(jnp.int32)
    match = jnp.concatenate([match, jnp.max(match, axis=0, keepdims=True)])
    match = jnp.concatenate([match, jnp.max(match, axis=1, keepdims=True)], axis=1)

    def renew(kept, go, slots=(), after=()):
        resent = len(slots)
        return pl.pallas_call(
            lambda *refs: renew_kernel(senders, owned, len(after), resent, *refs),
            out_shape=(slot,) * resent + (held,),
            in_specs=[SMEM] + [ANY] * (3 + senders + resent + len(after)),
            out_specs=(ANY,) * (resent + 1),
            scratch_shapes=[
                pltpu.VMEM((stored, width, width), dtype),
                pltpu.VMEM((stored, width, batches * shots), dtype),
                pltpu.VMEM((senders,) + tile, dtype),
                pltpu.VMEM(tile, jnp.float32),
                pltpu.VMEM((stored,) + tile, dtype),
                DMA((stored,)),
                DMA((stored, batches)),
                DMA((senders,)),
                DMA((stored,)),
                DMA((stored,)),
            ],
            input_output_aliases={3 + senders + at: at for at in range(resent + 1)},
            compiler_params=PARAMS,
            name="renew",
        )(jnp.concatenate([table, go[None], match.reshape(-1)]), source, blocks, *recv, *slots, kept, *after)

    traces = pl.pallas_call(
        lambda *refs: zero_kernel(owned, senders, stored, batches, *refs),
        out_shape=jax.ShapeDtypeStruct((batches, owned, width, shots), dtype),
        in_specs=[SMEM, ANY],
        out_specs=ANY,
        scratch_shapes=[pltpu.VMEM((width, shots), dtype), pltpu.SMEM((senders,), jnp.int32), DMA((batches, owned))],
        compiler_params=PARAMS,
        name="zeros",
    )(table, mine)

    *slots, kept = renew(kept, jnp.int32(1), tuple(slots), (traces,))

    def again(step, kept, down, top):
        sent = lax.dynamic_index_in_dim(kept, (place + step) % senders, 0, keepdims=False)
        return lax.ppermute(sent, AXES, pairs(step, down, top))

    def one_by_one(mask, send, came):
        def resend(carry):
            left, mask, came = carry
            step = jnp.argmax(mask).astype(jnp.int32)
            branches = [
                lambda came, step=step: came[:step] + (send(step),) + came[step + 1 :] for step in range(senders)
            ]
            return left - 1, jnp.where(steps == step, 0, mask), lax.switch(step, branches, came)

        return lax.while_loop(lambda carry: carry[0] > 0, resend, (jnp.sum(mask), mask, tuple(came)))[2]

    if masks:
        for low in range(0, senders, group):
            near = range(low, min(low + group, senders))

            def resend(which):
                return lambda new, old: tuple(
                    lax.ppermute(new[at], AXES, pairs(step, 1, 1)) if which >> at & 1 else old[at]
                    for at, step in enumerate(near)
                )

            code = sum(masks[0][step] << at for at, step in enumerate(near))
            recv[low : low + group] = lax.switch(
                code,
                [resend(which) for which in range(1 << len(near))],
                tuple(slots[low : low + group]),
                tuple(recv[low : low + group]),
            )
        (kept,) = renew(kept, jnp.where(depth >= 2, jnp.max(masks[0]), 0))
    arrived = lax.all_to_all(kept, "trace", split_axis=0, concat_axis=0, tiled=True)

    late = kept
    for wave, mask in enumerate(masks[1:], 3):
        recv = list(one_by_one(mask, lambda step, late=late, wave=wave: again(step, late, 1, wave - 1), recv))
        (late,) = renew(late, jnp.where(depth >= wave, jnp.max(mask), 0))
    fixes = one_by_one(late_mask, lambda step: again(step, late, 0, 0), recv)

    traces = pl.pallas_call(
        lambda *refs: write_kernel(owned, senders, stored, batches, *refs),
        out_shape=jax.ShapeDtypeStruct((batches, owned, width, shots), dtype),
        in_specs=[SMEM] + [ANY] * (senders + 2),
        out_specs=ANY,
        scratch_shapes=[
            pltpu.VMEM((senders,) + tile, dtype),
            pltpu.VMEM(tile, jnp.float32),
            pltpu.VMEM((senders,) + tile, dtype),
            pltpu.SMEM((senders,), jnp.int32),
            DMA((senders,)),
            DMA((senders, batches)),
        ],
        input_output_aliases={2 + senders: 0},
        compiler_params=PARAMS,
        name="write",
    )(jnp.concatenate([table, fixed]), arrived, *fixes, traces)
    return traces.reshape(1, batches, local, shots)


def solution(mesh):
    placed = (
        P("layer", "trace", None, None),
        P("layer", None, "trace", None),
        P("layer", None, None),
        P("layer", "trace", None),
    )
    return jax.shard_map(
        body, mesh=mesh, in_specs=placed, out_specs=P("layer", None, "trace", None), check_vma=False
    )
```

```python
import jax
import jax.numpy as jnp
from jax import lax
from jax.experimental import pallas as pl
from jax.experimental.pallas import tpu as pltpu
from jax.sharding import PartitionSpec as P


AXES = ("layer", "trace")
SMEM = pl.BlockSpec(memory_space=pltpu.SMEM)
ANY = pl.BlockSpec(memory_space=pl.ANY)
PARAMS = pltpu.CompilerParams(vmem_limit_bytes=67043328)
DMA = pltpu.SemaphoreType.DMA


def owner_of(row, owned):
    if owned & (owned - 1) == 0:
        return lax.shift_right_logical(row, jnp.int32(owned.bit_length() - 1))
    return lax.div(row, jnp.int32(owned))


def read_table(table, senders, stored):
    held = senders * stored

    def rows(sender, block):
        return table[sender * stored + block]

    def cols(block):
        return table[held + block]

    def more(at):
        return table[held + stored + 1 + at]

    return rows, cols, table[held + stored], more


def first_kernel(senders, owned, rows_ref, cols_ref, source, blocks, *refs):
    slots, refs = refs[:senders], refs[senders:]
    kept, operand, pieces, made, op_sem, in_sem, slot_sem, keep_sem = refs
    stored, _ = blocks.shape[:2]
    place = lax.axis_index("trace")
    batches, shots = source.shape[0], source.shape[-1]

    def rows(sender, block):
        return rows_ref[0, sender, block]

    def load(block):
        return pltpu.make_async_copy(blocks.at[block], operand.at[block], op_sem.at[block])

    def fetch(block, batch):
        return pltpu.make_async_copy(
            source.at[batch, cols_ref[0, 0, block] - place * owned],
            pieces.at[block, :, pl.ds(batch * shots, shots)],
            in_sem.at[block, batch],
        )

    def give(block, slot):
        return pltpu.make_async_copy(made.at[block], slots[slot], slot_sem.at[block])

    def keep(block, owner):
        return pltpu.make_async_copy(made.at[block], kept.at[owner], keep_sem.at[block])

    @pl.loop(0, stored)
    def _(block):
        for batch in range(batches):
            fetch(block, batch).start()
        load(block).start()

    @pl.loop(0, stored)
    def _(block):
        for batch in range(batches):
            fetch(block, batch).wait()
        load(block).wait()
        product = jnp.dot(operand[block], pieces[block], preferred_element_type=jnp.float32)
        for batch in range(batches):
            made[block, batch] = product[:, batch * shots : (batch + 1) * shots].astype(made.dtype)
        owner = owner_of(rows(place, block), owned)
        shift = lax.rem(owner - place + senders, senders)
        for slot in range(senders):

            @pl.when(shift == slot)
            def _():
                give(block, slot).start()

        keep(block, owner).start()

    @pl.loop(0, stored)
    def _(block):
        give(block, 0).wait()
        keep(block, 0).wait()


def renew_kernel(senders, owned, others, resent, table, source, blocks, *refs):
    recv, refs = refs[:senders], refs[senders + 1 + resent + others :]
    slots, refs = refs[:resent], refs[resent:]
    kept, operand, pieces, arrived, total, made, op_sem, in_sem, recv_sem, keep_sem, slot_sem = refs
    stored, _ = blocks.shape[:2]
    rows, cols, place, more = read_table(table, senders, stored)
    go = more(0) > 0

    def match(block, sender):
        return more(1 + block * (senders + 1) + sender)

    batches, shots = source.shape[0], source.shape[-1]

    def load(block):
        return pltpu.make_async_copy(blocks.at[block], operand.at[block], op_sem.at[block])

    def fetch(block, batch):
        return pltpu.make_async_copy(
            source.at[batch, cols(block) - place * owned],
            pieces.at[block, :, pl.ds(batch * shots, shots)],
            in_sem.at[block, batch],
        )

    def take(step):
        return pltpu.make_async_copy(recv[step], arrived.at[step], recv_sem.at[step])

    def keep(block, owner):
        return pltpu.make_async_copy(made.at[block], kept.at[owner], keep_sem.at[block])

    def give(block, slot):
        return pltpu.make_async_copy(made.at[block], slots[slot], slot_sem.at[block])

    def hits(block):
        return match(block, senders)

    def sender_at(step):
        return lax.rem(place - step + senders, senders)

    @pl.when(go)
    def _():
        for step in range(senders):

            @pl.when(match(stored, sender_at(step)) > 0)
            def _():
                take(step).start()

        @pl.loop(0, stored)
        def _(block):
            @pl.when(hits(block) > 0)
            def _():
                for batch in range(batches):
                    fetch(block, batch).start()
                load(block).start()

        for step in range(senders):

            @pl.when(match(stored, sender_at(step)) > 0)
            def _():
                take(step).wait()

        @pl.loop(0, stored)
        def _(block):
            @pl.when(hits(block) > 0)
            def _():
                total[...] = jnp.zeros_like(total)

                @pl.loop(0, senders)
                def _(step):
                    @pl.when(match(block, sender_at(step)) > 0)
                    def _():
                        total[...] += arrived[step].astype(jnp.float32)

                for batch in range(batches):
                    fetch(block, batch).wait()
                for batch in range(batches):
                    lanes = pl.ds(batch * shots, shots)
                    incoming = total[batch].astype(pieces.dtype).astype(jnp.float32)
                    pieces[block, :, lanes] = (
                        incoming + pieces[block, :, lanes].astype(jnp.float32)
                    ).astype(pieces.dtype)
                load(block).wait()
                product = jnp.dot(operand[block], pieces[block], preferred_element_type=jnp.float32)
                for batch in range(batches):
                    made[block, batch] = product[:, batch * shots : (batch + 1) * shots].astype(made.dtype)
                owner = owner_of(rows(place, block), owned)
                keep(block, owner).start()
                for slot in range(resent):

                    @pl.when(lax.rem(owner - place + senders, senders) == slot)
                    def _():
                        give(block, slot).start()

        @pl.loop(0, stored)
        def _(block):
            @pl.when(hits(block) > 0)
            def _():
                keep(block, 0).wait()
                if resent:
                    give(block, 0).wait()


def hit_rows(rows, senders, place, owned, stored, here):
    first = place * owned

    @pl.loop(0, senders)
    def _(sender):
        row = jnp.int32(-1)
        for other in range(stored):
            value = rows(sender, other) - first
            row = jnp.where((value >= 0) & (value < owned), value, row)
        here[sender] = row


def zero_kernel(owned, senders, stored, batches, table, after, out, nothing, here, sem):
    rows, _, place, _ = read_table(table, senders, stored)
    hit_rows(rows, senders, place, owned, stored, here)
    nothing[...] = jnp.zeros_like(nothing)

    def free(row):
        total = jnp.int32(0)
        for sender in range(senders):
            total += (here[sender] == row).astype(jnp.int32)
        return total == 0

    def put(batch, row):
        return pltpu.make_async_copy(nothing, out.at[batch, row], sem.at[batch, row])

    @pl.loop(0, owned)
    def _(row):
        @pl.when(free(row))
        def _():
            for batch in range(batches):
                put(batch, row).start()

    @pl.loop(0, owned)
    def _(row):
        @pl.when(free(row))
        def _():
            for batch in range(batches):
                put(batch, row).wait()


def write_kernel(owned, senders, stored, batches, table, recv, *refs):
    _, out, arrived, total, made, here, in_sem, out_sem = refs
    rows, _, place, _ = read_table(table, senders, stored)
    hit_rows(rows, senders, place, owned, stored, here)

    def take(sender):
        return pltpu.make_async_copy(recv.at[sender], arrived.at[sender], in_sem.at[sender])

    def put(sender, batch, box):
        return pltpu.make_async_copy(box.at[sender, batch], out.at[batch, here[sender]], out_sem.at[sender, batch])

    def count(sender, first, last):
        total = jnp.int32(0)
        for other in range(senders):
            same = (here[other] == here[sender]) & (other >= first) & (other < last)
            total += same.astype(jnp.int32)
        return total

    @pl.loop(0, senders)
    def _(sender):
        @pl.when(here[sender] >= 0)
        def _():
            take(sender).start()

    @pl.loop(0, senders)
    def _(sender):
        @pl.when(here[sender] >= 0)
        def _():
            take(sender).wait()

    @pl.loop(0, senders)
    def _(sender):
        @pl.when((here[sender] >= 0) & (count(sender, 0, sender) == 0))
        def _():
            more = count(sender, sender + 1, senders)

            @pl.when(more == 0)
            def _():
                for batch in range(batches):
                    put(sender, batch, arrived).start()

            @pl.when(more > 0)
            def _():
                total[...] = arrived[sender].astype(jnp.float32)

                @pl.loop(sender + 1, senders)
                def _(other):
                    @pl.when(here[other] == here[sender])
                    def _():
                        total[...] += arrived[other].astype(jnp.float32)

                made[sender] = total[...].astype(made.dtype)
                for batch in range(batches):
                    put(sender, batch, made).start()

    @pl.loop(0, senders)
    def _(sender):
        @pl.when((here[sender] >= 0) & (count(sender, 0, sender) == 0))
        def _():
            for batch in range(batches):
                put(sender, batch, made).wait()


def body(operators, sources, row_block, col_block):
    place = lax.axis_index("trace")
    depth = lax.axis_index("layer")
    senders = lax.axis_size("trace")
    layers = lax.axis_size("layer")
    blocks = operators[0]
    rows = row_block[0]
    stored, width = blocks.shape[0], blocks.shape[-1]
    batches, local, shots = sources.shape[1:]
    owned = local // width
    source = sources.reshape(batches, owned, width, shots)
    cols = col_block[0, 0]
    table = jnp.concatenate([rows.reshape(-1), cols, place[None].astype(jnp.int32)])
    dtype = sources.dtype
    tile = (batches, width, shots)
    slot = jax.ShapeDtypeStruct(tile, dtype)
    held = jax.ShapeDtypeStruct((senders,) + tile, dtype)

    def pairs(step, top=0):
        return [
            (i * senders + j, (i + 1) * senders + (j + step) % senders)
            for i in range(top, layers - 1)
            for j in range(senders)
        ]

    *slots, kept = pl.pallas_call(
        lambda *refs: first_kernel(senders, owned, *refs),
        out_shape=(slot,) * senders + (held,),
        in_specs=[SMEM] * 2 + [ANY] * 2,
        out_specs=(ANY,) * (senders + 1),
        scratch_shapes=[
            pltpu.VMEM((stored, width, width), dtype),
            pltpu.VMEM((stored, width, batches * shots), dtype),
            pltpu.VMEM((stored,) + tile, dtype),
            DMA((stored,)),
            DMA((stored, batches)),
            DMA((stored,)),
            DMA((stored,)),
        ],
        compiler_params=PARAMS,
        name="first",
    )(row_block, col_block, source, blocks)
    recv = [None] * senders
    for step in sorted(range(senders), key=lambda step: abs(2 * step - senders)):
        recv[step] = lax.ppermute(slots[step], AXES, pairs(step))

    total = layers * senders
    mine, kept = lax.optimization_barrier((table, kept))
    mine = jnp.broadcast_to(mine[None], (total, mine.shape[0]))
    known = lax.all_to_all(mine, AXES, split_axis=0, concat_axis=0, tiled=True)
    known = known.reshape(layers, senders, -1)
    blocks_all = senders * stored
    rows_all = known[:, 0, :blocks_all]
    cols_all = known[:, :, blocks_all : blocks_all + stored].reshape(layers, blocks_all)
    feeds = rows_all[:-1, :, None] == cols_all[1:, None, :]
    read = jnp.any(feeds, axis=2)
    home = jnp.repeat(jnp.arange(senders, dtype=jnp.int32), stored)
    shift = (rows_all[:-1] // owned - home[None, :]) % senders
    steps = jnp.arange(senders, dtype=jnp.int32)
    changed = jnp.any(feeds, axis=1)
    masks = []
    for wave in range(2, layers):
        below = jnp.concatenate([jnp.zeros((1, blocks_all), bool), changed[:-1]])
        again = below & read
        mask = jnp.any(again[:, :, None] & (shift[:, :, None] == steps), axis=(0, 1)).astype(jnp.int32)
        masks.append(mask)
        changed = jnp.any(feeds & below[:, :, None], axis=1)

    above = lax.dynamic_index_in_dim(rows_all, jnp.maximum(depth - 1, 0), 0, keepdims=False)
    above = above.reshape(senders, stored)
    match = jnp.any((above[None] == cols[:, None, None]) & (depth > 0), axis=2).astype(jnp.int32)
    match = jnp.concatenate([match, jnp.max(match, axis=0, keepdims=True)])
    match = jnp.concatenate([match, jnp.max(match, axis=1, keepdims=True)], axis=1)

    def renew(kept, go, slots=(), after=()):
        resent = len(slots)
        return pl.pallas_call(
            lambda *refs: renew_kernel(senders, owned, len(after), resent, *refs),
            out_shape=(slot,) * resent + (held,),
            in_specs=[SMEM] + [ANY] * (3 + senders + resent + len(after)),
            out_specs=(ANY,) * (resent + 1),
            scratch_shapes=[
                pltpu.VMEM((stored, width, width), dtype),
                pltpu.VMEM((stored, width, batches * shots), dtype),
                pltpu.VMEM((senders,) + tile, dtype),
                pltpu.VMEM(tile, jnp.float32),
                pltpu.VMEM((stored,) + tile, dtype),
                DMA((stored,)),
                DMA((stored, batches)),
                DMA((senders,)),
                DMA((stored,)),
                DMA((stored,)),
            ],
            input_output_aliases={3 + senders + at: at for at in range(resent + 1)},
            compiler_params=PARAMS,
            name="renew",
        )(jnp.concatenate([table, go[None], match.reshape(-1)]), source, blocks, *recv, *slots, kept, *after)

    traces = pl.pallas_call(
        lambda *refs: zero_kernel(owned, senders, stored, batches, *refs),
        out_shape=jax.ShapeDtypeStruct((batches, owned, width, shots), dtype),
        in_specs=[SMEM, ANY],
        out_specs=ANY,
        scratch_shapes=[
            pltpu.VMEM((width, shots), dtype),
            pltpu.SMEM((senders,), jnp.int32),
            DMA((batches, owned)),
        ],
        compiler_params=PARAMS,
        name="zeros",
    )(table, mine)

    *slots, kept = renew(kept, jnp.int32(1), tuple(slots), (traces,))
    for wave, mask in enumerate(masks, 2):
        group = 4 if wave == 2 and senders <= 8 else 2
        for low in range(0, senders, group):
            near = range(low, min(low + group, senders))

            def resend(which):
                return lambda new, old: tuple(
                    lax.ppermute(new[at], AXES, pairs(step, wave - 1)) if which >> at & 1 else old[at]
                    for at, step in enumerate(near)
                )

            code = sum(mask[step] << at for at, step in enumerate(near))
            recv[low : low + group] = lax.switch(
                code,
                [resend(which) for which in range(1 << len(near))],
                tuple(slots[low : low + group]),
                tuple(recv[low : low + group]),
            )
        go = jnp.where(depth >= wave, jnp.max(mask), 0)
        *slots, kept = renew(kept, go, tuple(slots) if wave + 1 < layers else ())
    arrived = lax.all_to_all(kept, "trace", split_axis=0, concat_axis=0, tiled=True)

    traces = pl.pallas_call(
        lambda *refs: write_kernel(owned, senders, stored, batches, *refs),
        out_shape=jax.ShapeDtypeStruct((batches, owned, width, shots), dtype),
        in_specs=[SMEM] + [ANY] * 2,
        out_specs=ANY,
        scratch_shapes=[
            pltpu.VMEM((senders,) + tile, dtype),
            pltpu.VMEM(tile, jnp.float32),
            pltpu.VMEM((senders,) + tile, dtype),
            pltpu.SMEM((senders,), jnp.int32),
            DMA((senders,)),
            DMA((senders, batches)),
        ],
        input_output_aliases={2: 0},
        compiler_params=PARAMS,
        name="write",
    )(table, arrived, traces)
    return traces.reshape(1, batches, local, shots)


def solution(mesh):
    placed = (
        P("layer", "trace", None, None),
        P("layer", None, "trace", None),
        P("layer", None, None),
        P("layer", "trace", None),
    )
    return jax.shard_map(
        body, mesh=mesh, in_specs=placed, out_specs=P("layer", None, "trace", None), check_vma=False
    )
```

```python
import jax
import jax.numpy as jnp
from jax import lax
from jax.experimental import pallas as pl
from jax.experimental.pallas import tpu as pltpu
from jax.sharding import PartitionSpec as P


AXES = ("layer", "trace")
SMEM = pl.BlockSpec(memory_space=pltpu.SMEM)
ANY = pl.BlockSpec(memory_space=pl.ANY)
PARAMS = pltpu.CompilerParams(vmem_limit_bytes=67043328)
DMA = pltpu.SemaphoreType.DMA


def owner_of(row, owned):
    if owned & (owned - 1) == 0:
        return lax.shift_right_logical(row, jnp.int32(owned.bit_length() - 1))
    return lax.div(row, jnp.int32(owned))


def read_table(table, senders, stored):
    held = senders * stored

    def rows(sender, block):
        return table[sender * stored + block]

    def cols(block):
        return table[held + block]

    def more(at):
        return table[held + stored + 1 + at]

    return rows, cols, table[held + stored], more


def first_kernel(senders, owned, rows_ref, cols_ref, source, blocks, *refs):
    slots, refs = refs[:senders], refs[senders:]
    operand, pieces, made, op_sem, in_sem, slot_sem = refs
    stored, _ = blocks.shape[:2]
    place = lax.axis_index("trace")
    batches, shots = source.shape[0], source.shape[-1]

    def rows(sender, block):
        return rows_ref[0, sender, block]

    def load(block):
        return pltpu.make_async_copy(blocks.at[block], operand.at[block], op_sem.at[block])

    def fetch(block, batch):
        return pltpu.make_async_copy(
            source.at[batch, cols_ref[0, 0, block] - place * owned],
            pieces.at[block, :, pl.ds(batch * shots, shots)],
            in_sem.at[block, batch],
        )

    def give(block, slot):
        return pltpu.make_async_copy(made.at[block], slots[slot], slot_sem.at[block])

    @pl.loop(0, stored)
    def _(block):
        for batch in range(batches):
            fetch(block, batch).start()
        load(block).start()

    @pl.loop(0, stored)
    def _(block):
        for batch in range(batches):
            fetch(block, batch).wait()
        load(block).wait()
        product = jnp.dot(operand[block], pieces[block], preferred_element_type=jnp.float32)
        for batch in range(batches):
            made[block, batch] = product[:, batch * shots : (batch + 1) * shots].astype(made.dtype)
        owner = owner_of(rows(place, block), owned)
        shift = lax.rem(owner - place + senders, senders)
        for slot in range(senders):

            @pl.when(shift == slot)
            def _():
                give(block, slot).start()

    @pl.loop(0, stored)
    def _(block):
        give(block, 0).wait()


def renew_kernel(senders, owned, others, table, source, blocks, *refs):
    recv, refs = refs[:senders], refs[2 * senders + others :]
    slots, refs = refs[:senders], refs[senders:]
    operand, pieces, arrived, total, made, op_sem, in_sem, recv_sem, slot_sem = refs
    stored, _ = blocks.shape[:2]
    rows, cols, place, more = read_table(table, senders, stored)
    go = more(0) > 0

    def match(block, sender):
        return more(1 + block * (senders + 1) + sender)

    batches, shots = source.shape[0], source.shape[-1]

    def load(block):
        return pltpu.make_async_copy(blocks.at[block], operand.at[block], op_sem.at[block])

    def fetch(block, batch):
        return pltpu.make_async_copy(
            source.at[batch, cols(block) - place * owned],
            pieces.at[block, :, pl.ds(batch * shots, shots)],
            in_sem.at[block, batch],
        )

    def take(step):
        return pltpu.make_async_copy(recv[step], arrived.at[step], recv_sem.at[step])

    def give(block, slot):
        return pltpu.make_async_copy(made.at[block], slots[slot], slot_sem.at[block])

    def hits(block):
        return match(block, senders)

    def sender_at(step):
        return lax.rem(place - step + senders, senders)

    @pl.when(go)
    def _():
        for step in range(senders):

            @pl.when(match(stored, sender_at(step)) > 0)
            def _():
                take(step).start()

        @pl.loop(0, stored)
        def _(block):
            @pl.when(hits(block) > 0)
            def _():
                for batch in range(batches):
                    fetch(block, batch).start()
                load(block).start()

        for step in range(senders):

            @pl.when(match(stored, sender_at(step)) > 0)
            def _():
                take(step).wait()

        @pl.loop(0, stored)
        def _(block):
            @pl.when(hits(block) > 0)
            def _():
                total[...] = jnp.zeros_like(total)

                @pl.loop(0, senders)
                def _(step):
                    @pl.when(match(block, sender_at(step)) > 0)
                    def _():
                        total[...] += arrived[step].astype(jnp.float32)

                for batch in range(batches):
                    fetch(block, batch).wait()
                for batch in range(batches):
                    lanes = pl.ds(batch * shots, shots)
                    incoming = total[batch].astype(pieces.dtype).astype(jnp.float32)
                    pieces[block, :, lanes] = (
                        incoming + pieces[block, :, lanes].astype(jnp.float32)
                    ).astype(pieces.dtype)
                load(block).wait()
                product = jnp.dot(operand[block], pieces[block], preferred_element_type=jnp.float32)
                for batch in range(batches):
                    made[block, batch] = product[:, batch * shots : (batch + 1) * shots].astype(made.dtype)
                owner = owner_of(rows(place, block), owned)
                for slot in range(senders):

                    @pl.when(lax.rem(owner - place + senders, senders) == slot)
                    def _():
                        give(block, slot).start()

        @pl.loop(0, stored)
        def _(block):
            @pl.when(hits(block) > 0)
            def _():
                give(block, 0).wait()


def hit_rows(rows, senders, place, owned, stored, here):
    first = place * owned

    @pl.loop(0, senders)
    def _(sender):
        row = jnp.int32(-1)
        for other in range(stored):
            value = rows(sender, other) - first
            row = jnp.where((value >= 0) & (value < owned), value, row)
        here[sender] = row


def zero_kernel(owned, senders, stored, batches, table, after, out, nothing, here, sem):
    rows, _, place, _ = read_table(table, senders, stored)
    hit_rows(rows, senders, place, owned, stored, here)
    nothing[...] = jnp.zeros_like(nothing)

    def free(row):
        total = jnp.int32(0)
        for sender in range(senders):
            total += (here[sender] == row).astype(jnp.int32)
        return total == 0

    def put(batch, row):
        return pltpu.make_async_copy(nothing, out.at[batch, row], sem.at[batch, row])

    @pl.loop(0, owned)
    def _(row):
        @pl.when(free(row))
        def _():
            for batch in range(batches):
                put(batch, row).start()

    @pl.loop(0, owned)
    def _(row):
        @pl.when(free(row))
        def _():
            for batch in range(batches):
                put(batch, row).wait()


def write_kernel(owned, senders, stored, batches, table, *refs):
    recv, refs = refs[:senders], refs[senders + 1 :]
    out, arrived, total, made, here, in_sem, out_sem = refs
    rows, _, place, _ = read_table(table, senders, stored)
    hit_rows(rows, senders, place, owned, stored, here)

    def take(step, sender):
        return pltpu.make_async_copy(recv[step], arrived.at[sender], in_sem.at[sender])

    def put(sender, batch, box):
        return pltpu.make_async_copy(box.at[sender, batch], out.at[batch, here[sender]], out_sem.at[sender, batch])

    def count(sender, first, last):
        total = jnp.int32(0)
        for other in range(senders):
            same = (here[other] == here[sender]) & (other >= first) & (other < last)
            total += same.astype(jnp.int32)
        return total

    for step in range(senders):
        sender = lax.rem(place - step + senders, senders)

        @pl.when(here[sender] >= 0)
        def _():
            take(step, sender).start()

    @pl.loop(0, senders)
    def _(sender):
        @pl.when(here[sender] >= 0)
        def _():
            take(0, sender).wait()

    @pl.loop(0, senders)
    def _(sender):
        @pl.when((here[sender] >= 0) & (count(sender, 0, sender) == 0))
        def _():
            more = count(sender, sender + 1, senders)

            @pl.when(more == 0)
            def _():
                for batch in range(batches):
                    put(sender, batch, arrived).start()

            @pl.when(more > 0)
            def _():
                total[...] = arrived[sender].astype(jnp.float32)

                @pl.loop(sender + 1, senders)
                def _(other):
                    @pl.when(here[other] == here[sender])
                    def _():
                        total[...] += arrived[other].astype(jnp.float32)

                made[sender] = total[...].astype(made.dtype)
                for batch in range(batches):
                    put(sender, batch, made).start()

    @pl.loop(0, senders)
    def _(sender):
        @pl.when((here[sender] >= 0) & (count(sender, 0, sender) == 0))
        def _():
            for batch in range(batches):
                put(sender, batch, made).wait()


def body(operators, sources, row_block, col_block):
    place = lax.axis_index("trace")
    depth = lax.axis_index("layer")
    senders = lax.axis_size("trace")
    layers = lax.axis_size("layer")
    blocks = operators[0]
    rows = row_block[0]
    stored, width = blocks.shape[0], blocks.shape[-1]
    batches, local, shots = sources.shape[1:]
    owned = local // width
    source = sources.reshape(batches, owned, width, shots)
    cols = col_block[0, 0]
    table = jnp.concatenate([rows.reshape(-1), cols, place[None].astype(jnp.int32)])
    dtype = sources.dtype
    tile = (batches, width, shots)
    slot = jax.ShapeDtypeStruct(tile, dtype)

    def pairs(step, top=0):
        return [
            (i * senders + j, (i + 1) * senders + (j + step) % senders)
            for i in range(top, layers - 1)
            for j in range(senders)
        ]

    slots = pl.pallas_call(
        lambda *refs: first_kernel(senders, owned, *refs),
        out_shape=(slot,) * senders,
        in_specs=[SMEM] * 2 + [ANY] * 2,
        out_specs=(ANY,) * senders,
        scratch_shapes=[
            pltpu.VMEM((stored, width, width), dtype),
            pltpu.VMEM((stored, width, batches * shots), dtype),
            pltpu.VMEM((stored,) + tile, dtype),
            DMA((stored,)),
            DMA((stored, batches)),
            DMA((stored,)),
        ],
        compiler_params=PARAMS,
        name="first",
    )(row_block, col_block, source, blocks)
    recv = [None] * senders
    for step in sorted(range(senders), key=lambda step: abs(2 * step - senders)):
        recv[step] = lax.ppermute(slots[step], AXES, pairs(step))

    total = layers * senders
    mine, slots = lax.optimization_barrier((table, slots))
    mine = jnp.broadcast_to(mine[None], (total, mine.shape[0]))
    known = lax.all_to_all(mine, AXES, split_axis=0, concat_axis=0, tiled=True)
    known = known.reshape(layers, senders, -1)
    blocks_all = senders * stored
    rows_all = known[:, 0, :blocks_all]
    cols_all = known[:, :, blocks_all : blocks_all + stored].reshape(layers, blocks_all)
    feeds = rows_all[:-1, :, None] == cols_all[1:, None, :]
    read = jnp.any(feeds, axis=2)
    home = jnp.repeat(jnp.arange(senders, dtype=jnp.int32), stored)
    shift = (rows_all[:-1] // owned - home[None, :]) % senders
    steps = jnp.arange(senders, dtype=jnp.int32)
    changed = jnp.any(feeds, axis=1)
    masks = []
    for wave in range(2, layers):
        below = jnp.concatenate([jnp.zeros((1, blocks_all), bool), changed[:-1]])
        again = below & read
        mask = jnp.any(again[:, :, None] & (shift[:, :, None] == steps), axis=(0, 1)).astype(jnp.int32)
        masks.append(mask)
        changed = jnp.any(feeds & below[:, :, None], axis=1)

    above = lax.dynamic_index_in_dim(rows_all, jnp.maximum(depth - 1, 0), 0, keepdims=False)
    above = above.reshape(senders, stored)
    match = jnp.any((above[None] == cols[:, None, None]) & (depth > 0), axis=2).astype(jnp.int32)
    match = jnp.concatenate([match, jnp.max(match, axis=0, keepdims=True)])
    match = jnp.concatenate([match, jnp.max(match, axis=1, keepdims=True)], axis=1)

    def renew(slots, go, after=()):
        return pl.pallas_call(
            lambda *refs: renew_kernel(senders, owned, len(after), *refs),
            out_shape=(slot,) * senders,
            in_specs=[SMEM] + [ANY] * (2 + 2 * senders + len(after)),
            out_specs=(ANY,) * senders,
            scratch_shapes=[
                pltpu.VMEM((stored, width, width), dtype),
                pltpu.VMEM((stored, width, batches * shots), dtype),
                pltpu.VMEM((senders,) + tile, dtype),
                pltpu.VMEM(tile, jnp.float32),
                pltpu.VMEM((stored,) + tile, dtype),
                DMA((stored,)),
                DMA((stored, batches)),
                DMA((senders,)),
                DMA((stored,)),
            ],
            input_output_aliases={3 + senders + at: at for at in range(senders)},
            compiler_params=PARAMS,
            name="renew",
        )(jnp.concatenate([table, go[None], match.reshape(-1)]), source, blocks, *recv, *slots, *after)

    traces = pl.pallas_call(
        lambda *refs: zero_kernel(owned, senders, stored, batches, *refs),
        out_shape=jax.ShapeDtypeStruct((batches, owned, width, shots), dtype),
        in_specs=[SMEM, ANY],
        out_specs=ANY,
        scratch_shapes=[pltpu.VMEM((width, shots), dtype), pltpu.SMEM((senders,), jnp.int32), DMA((batches, owned))],
        compiler_params=PARAMS,
        name="zeros",
    )(table, mine)

    slots = renew(slots, jnp.int32(1), (traces,))
    for wave, mask in enumerate(masks, 2):
        group = 4 if wave == 2 and senders <= 8 else 2
        for low in range(0, senders, group):
            near = range(low, min(low + group, senders))

            def resend(which):
                return lambda new, old: tuple(
                    lax.ppermute(new[at], AXES, pairs(step, wave - 1)) if which >> at & 1 else old[at]
                    for at, step in enumerate(near)
                )

            code = sum(mask[step] << at for at, step in enumerate(near))
            recv[low : low + group] = lax.switch(
                code,
                [resend(which) for which in range(1 << len(near))],
                tuple(slots[low : low + group]),
                tuple(recv[low : low + group]),
            )
        go = jnp.where(depth >= wave, jnp.max(mask), 0)
        slots = renew(slots, go)
    arrived = [
        lax.ppermute(slots[step], "trace", [(j, (j + step) % senders) for j in range(senders)]) if step else slots[0]
        for step in range(senders)
    ]

    traces = pl.pallas_call(
        lambda *refs: write_kernel(owned, senders, stored, batches, *refs),
        out_shape=jax.ShapeDtypeStruct((batches, owned, width, shots), dtype),
        in_specs=[SMEM] + [ANY] * (senders + 1),
        out_specs=ANY,
        scratch_shapes=[
            pltpu.VMEM((senders,) + tile, dtype),
            pltpu.VMEM(tile, jnp.float32),
            pltpu.VMEM((senders,) + tile, dtype),
            pltpu.SMEM((senders,), jnp.int32),
            DMA((senders,)),
            DMA((senders, batches)),
        ],
        input_output_aliases={1 + senders: 0},
        compiler_params=PARAMS,
        name="write",
    )(table, *arrived, traces)
    return traces.reshape(1, batches, local, shots)


def solution(mesh):
    placed = (
        P("layer", "trace", None, None),
        P("layer", None, "trace", None),
        P("layer", None, None),
        P("layer", "trace", None),
    )
    return jax.shard_map(
        body, mesh=mesh, in_specs=placed, out_specs=P("layer", None, "trace", None), check_vma=False
    )
```

```python
import jax
import jax.numpy as jnp
from jax import lax
from jax.experimental import pallas as pl
from jax.experimental.pallas import tpu as pltpu
from jax.sharding import PartitionSpec as P


AXES = ("layer", "trace")
SMEM = pl.BlockSpec(memory_space=pltpu.SMEM)
ANY = pl.BlockSpec(memory_space=pl.ANY)
PARAMS = pltpu.CompilerParams(vmem_limit_bytes=67043328)
DMA = pltpu.SemaphoreType.DMA


def owner_of(row, owned):
    if owned & (owned - 1) == 0:
        return lax.shift_right_logical(row, jnp.int32(owned.bit_length() - 1))
    return lax.div(row, jnp.int32(owned))


def far_first(senders):
    return sorted(range(senders), key=lambda step: abs(2 * step - senders))


def read_table(table, senders, stored):
    held = senders * stored

    def rows(sender, block):
        return table[sender * stored + block]

    def cols(block):
        return table[held + block]

    def more(at):
        return table[held + stored + 1 + at]

    return rows, cols, table[held + stored], more


def first_kernel(senders, owned, rows_ref, cols_ref, source, blocks, *refs):
    slots, refs = refs[:senders], refs[senders:]
    operand, pieces, made, op_sem, in_sem, slot_sem = refs
    stored, _ = blocks.shape[:2]
    place = lax.axis_index("trace")
    batches, shots = source.shape[0], source.shape[-1]

    def rows(sender, block):
        return rows_ref[0, sender, block]

    def load(block):
        return pltpu.make_async_copy(blocks.at[block], operand.at[block], op_sem.at[block])

    def fetch(block, batch):
        return pltpu.make_async_copy(
            source.at[batch, cols_ref[0, 0, block] - place * owned],
            pieces.at[block, :, pl.ds(batch * shots, shots)],
            in_sem.at[block, batch],
        )

    def give(block, slot):
        return pltpu.make_async_copy(made.at[block], slots[slot], slot_sem.at[block])

    @pl.loop(0, stored)
    def _(block):
        for batch in range(batches):
            fetch(block, batch).start()
        load(block).start()

    @pl.loop(0, stored)
    def _(block):
        for batch in range(batches):
            fetch(block, batch).wait()
        load(block).wait()
        product = jnp.dot(operand[block], pieces[block], preferred_element_type=jnp.float32)
        for batch in range(batches):
            made[block, batch] = product[:, batch * shots : (batch + 1) * shots].astype(made.dtype)
        owner = owner_of(rows(place, block), owned)
        shift = lax.rem(owner - place + senders, senders)
        for slot in range(senders):

            @pl.when(shift == slot)
            def _():
                give(block, slot).start()

    @pl.loop(0, stored)
    def _(block):
        give(block, 0).wait()


def renew_kernel(senders, owned, others, table, source, blocks, *refs):
    recv, refs = refs[:senders], refs[2 * senders + others :]
    slots, refs = refs[:senders], refs[senders:]
    operand, pieces, arrived, total, made, op_sem, in_sem, recv_sem, slot_sem = refs
    stored, _ = blocks.shape[:2]
    rows, cols, place, more = read_table(table, senders, stored)
    go = more(0) > 0

    def match(block, sender):
        return more(1 + block * (senders + 1) + sender)

    batches, shots = source.shape[0], source.shape[-1]

    def load(block):
        return pltpu.make_async_copy(blocks.at[block], operand.at[block], op_sem.at[block])

    def fetch(block, batch):
        return pltpu.make_async_copy(
            source.at[batch, cols(block) - place * owned],
            pieces.at[block, :, pl.ds(batch * shots, shots)],
            in_sem.at[block, batch],
        )

    def take(step):
        return pltpu.make_async_copy(recv[step], arrived.at[step], recv_sem.at[step])

    def give(block, slot):
        return pltpu.make_async_copy(made.at[block], slots[slot], slot_sem.at[block])

    def hits(block):
        return match(block, senders)

    def sender_at(step):
        return lax.rem(place - step + senders, senders)

    @pl.when(go)
    def _():
        for step in range(senders):

            @pl.when(match(stored, sender_at(step)) > 0)
            def _():
                take(step).start()

        @pl.loop(0, stored)
        def _(block):
            @pl.when(hits(block) > 0)
            def _():
                for batch in range(batches):
                    fetch(block, batch).start()
                load(block).start()

        for step in range(senders):

            @pl.when(match(stored, sender_at(step)) > 0)
            def _():
                take(step).wait()

        @pl.loop(0, stored)
        def _(block):
            @pl.when(hits(block) > 0)
            def _():
                total[...] = jnp.zeros_like(total)

                @pl.loop(0, senders)
                def _(step):
                    @pl.when(match(block, sender_at(step)) > 0)
                    def _():
                        total[...] += arrived[step].astype(jnp.float32)

                for batch in range(batches):
                    fetch(block, batch).wait()
                for batch in range(batches):
                    lanes = pl.ds(batch * shots, shots)
                    incoming = total[batch].astype(pieces.dtype).astype(jnp.float32)
                    pieces[block, :, lanes] = (
                        incoming + pieces[block, :, lanes].astype(jnp.float32)
                    ).astype(pieces.dtype)
                load(block).wait()
                product = jnp.dot(operand[block], pieces[block], preferred_element_type=jnp.float32)
                for batch in range(batches):
                    made[block, batch] = product[:, batch * shots : (batch + 1) * shots].astype(made.dtype)
                owner = owner_of(rows(place, block), owned)
                for slot in range(senders):

                    @pl.when(lax.rem(owner - place + senders, senders) == slot)
                    def _():
                        give(block, slot).start()

        @pl.loop(0, stored)
        def _(block):
            @pl.when(hits(block) > 0)
            def _():
                give(block, 0).wait()


def hit_rows(rows, senders, place, owned, stored, here):
    first = place * owned

    @pl.loop(0, senders)
    def _(sender):
        row = jnp.int32(-1)
        for other in range(stored):
            value = rows(sender, other) - first
            row = jnp.where((value >= 0) & (value < owned), value, row)
        here[sender] = row


def zero_kernel(owned, senders, stored, batches, table, after, out, nothing, here, sem):
    rows, _, place, _ = read_table(table, senders, stored)
    hit_rows(rows, senders, place, owned, stored, here)
    nothing[...] = jnp.zeros_like(nothing)

    def free(row):
        total = jnp.int32(0)
        for sender in range(senders):
            total += (here[sender] == row).astype(jnp.int32)
        return total == 0

    def put(batch, row):
        return pltpu.make_async_copy(nothing, out.at[batch, row], sem.at[batch, row])

    @pl.loop(0, owned)
    def _(row):
        @pl.when(free(row))
        def _():
            for batch in range(batches):
                put(batch, row).start()

    @pl.loop(0, owned)
    def _(row):
        @pl.when(free(row))
        def _():
            for batch in range(batches):
                put(batch, row).wait()


def write_kernel(owned, senders, stored, batches, table, *refs):
    recv, refs = refs[:senders], refs[senders + 1 :]
    out, arrived, total, made, here, in_sem, out_sem = refs
    rows, _, place, _ = read_table(table, senders, stored)
    hit_rows(rows, senders, place, owned, stored, here)

    def take(step, sender):
        return pltpu.make_async_copy(recv[step], arrived.at[sender], in_sem.at[sender])

    def put(sender, batch, box):
        return pltpu.make_async_copy(box.at[sender, batch], out.at[batch, here[sender]], out_sem.at[sender, batch])

    def count(sender, first, last):
        total = jnp.int32(0)
        for other in range(senders):
            same = (here[other] == here[sender]) & (other >= first) & (other < last)
            total += same.astype(jnp.int32)
        return total

    for step in range(senders):
        sender = lax.rem(place - step + senders, senders)

        @pl.when(here[sender] >= 0)
        def _():
            take(step, sender).start()

    @pl.loop(0, senders)
    def _(sender):
        @pl.when(here[sender] >= 0)
        def _():
            take(0, sender).wait()

    @pl.loop(0, senders)
    def _(sender):
        @pl.when((here[sender] >= 0) & (count(sender, 0, sender) == 0))
        def _():
            more = count(sender, sender + 1, senders)

            @pl.when(more == 0)
            def _():
                for batch in range(batches):
                    put(sender, batch, arrived).start()

            @pl.when(more > 0)
            def _():
                total[...] = arrived[sender].astype(jnp.float32)

                @pl.loop(sender + 1, senders)
                def _(other):
                    @pl.when(here[other] == here[sender])
                    def _():
                        total[...] += arrived[other].astype(jnp.float32)

                made[sender] = total[...].astype(made.dtype)
                for batch in range(batches):
                    put(sender, batch, made).start()

    @pl.loop(0, senders)
    def _(sender):
        @pl.when((here[sender] >= 0) & (count(sender, 0, sender) == 0))
        def _():
            for batch in range(batches):
                put(sender, batch, made).wait()


def body(operators, sources, row_block, col_block):
    place = lax.axis_index("trace")
    depth = lax.axis_index("layer")
    senders = lax.axis_size("trace")
    layers = lax.axis_size("layer")
    blocks = operators[0]
    rows = row_block[0]
    stored, width = blocks.shape[0], blocks.shape[-1]
    batches, local, shots = sources.shape[1:]
    owned = local // width
    source = sources.reshape(batches, owned, width, shots)
    cols = col_block[0, 0]
    table = jnp.concatenate([rows.reshape(-1), cols, place[None].astype(jnp.int32)])
    dtype = sources.dtype
    tile = (batches, width, shots)
    slot = jax.ShapeDtypeStruct(tile, dtype)

    def pairs(step, top=0):
        return [
            (i * senders + j, (i + 1) * senders + (j + step) % senders)
            for i in range(top, layers - 1)
            for j in range(senders)
        ]

    slots = pl.pallas_call(
        lambda *refs: first_kernel(senders, owned, *refs),
        out_shape=(slot,) * senders,
        in_specs=[SMEM] * 2 + [ANY] * 2,
        out_specs=(ANY,) * senders,
        scratch_shapes=[
            pltpu.VMEM((stored, width, width), dtype),
            pltpu.VMEM((stored, width, batches * shots), dtype),
            pltpu.VMEM((stored,) + tile, dtype),
            DMA((stored,)),
            DMA((stored, batches)),
            DMA((stored,)),
        ],
        compiler_params=PARAMS,
        name="first",
    )(row_block, col_block, source, blocks)
    recv = [None] * senders
    for step in far_first(senders):
        recv[step] = lax.ppermute(slots[step], AXES, pairs(step))

    total = layers * senders
    mine, slots = lax.optimization_barrier((table, slots))
    mine = jnp.broadcast_to(mine[None], (total, mine.shape[0]))
    known = lax.all_to_all(mine, AXES, split_axis=0, concat_axis=0, tiled=True)
    known = known.reshape(layers, senders, -1)
    blocks_all = senders * stored
    rows_all = known[:, 0, :blocks_all]
    cols_all = known[:, :, blocks_all : blocks_all + stored].reshape(layers, blocks_all)
    feeds = rows_all[:-1, :, None] == cols_all[1:, None, :]
    read = jnp.any(feeds, axis=2)
    home = jnp.repeat(jnp.arange(senders, dtype=jnp.int32), stored)
    shift = (rows_all[:-1] // owned - home[None, :]) % senders
    steps = jnp.arange(senders, dtype=jnp.int32)
    changed = jnp.any(feeds, axis=1)
    masks = []
    for wave in range(2, layers):
        below = jnp.concatenate([jnp.zeros((1, blocks_all), bool), changed[:-1]])
        again = below & read
        mask = jnp.any(again[:, :, None] & (shift[:, :, None] == steps), axis=(0, 1)).astype(jnp.int32)
        masks.append(mask)
        changed = jnp.any(feeds & below[:, :, None], axis=1)

    above = lax.dynamic_index_in_dim(rows_all, jnp.maximum(depth - 1, 0), 0, keepdims=False)
    above = above.reshape(senders, stored)
    match = jnp.any((above[None] == cols[:, None, None]) & (depth > 0), axis=2).astype(jnp.int32)
    match = jnp.concatenate([match, jnp.max(match, axis=0, keepdims=True)])
    match = jnp.concatenate([match, jnp.max(match, axis=1, keepdims=True)], axis=1)

    def renew(slots, go, after=()):
        return pl.pallas_call(
            lambda *refs: renew_kernel(senders, owned, len(after), *refs),
            out_shape=(slot,) * senders,
            in_specs=[SMEM] + [ANY] * (2 + 2 * senders + len(after)),
            out_specs=(ANY,) * senders,
            scratch_shapes=[
                pltpu.VMEM((stored, width, width), dtype),
                pltpu.VMEM((stored, width, batches * shots), dtype),
                pltpu.VMEM((senders,) + tile, dtype),
                pltpu.VMEM(tile, jnp.float32),
                pltpu.VMEM((stored,) + tile, dtype),
                DMA((stored,)),
                DMA((stored, batches)),
                DMA((senders,)),
                DMA((stored,)),
            ],
            input_output_aliases={3 + senders + at: at for at in range(senders)},
            compiler_params=PARAMS,
            name="renew",
        )(jnp.concatenate([table, go[None], match.reshape(-1)]), source, blocks, *recv, *slots, *after)

    traces = pl.pallas_call(
        lambda *refs: zero_kernel(owned, senders, stored, batches, *refs),
        out_shape=jax.ShapeDtypeStruct((batches, owned, width, shots), dtype),
        in_specs=[SMEM, ANY],
        out_specs=ANY,
        scratch_shapes=[pltpu.VMEM((width, shots), dtype), pltpu.SMEM((senders,), jnp.int32), DMA((batches, owned))],
        compiler_params=PARAMS,
        name="zeros",
    )(table, mine)

    slots = renew(slots, jnp.int32(1), (traces,))
    for wave, mask in enumerate(masks, 2):
        group = 4 if wave == 2 and senders <= 8 else 2
        for low in range(0, senders, group):
            near = range(low, min(low + group, senders))

            def resend(which):
                return lambda new, old: tuple(
                    lax.ppermute(new[at], AXES, pairs(step, wave - 1)) if which >> at & 1 else old[at]
                    for at, step in enumerate(near)
                )

            code = sum(mask[step] << at for at, step in enumerate(near))
            recv[low : low + group] = lax.switch(
                code,
                [resend(which) for which in range(1 << len(near))],
                tuple(slots[low : low + group]),
                tuple(recv[low : low + group]),
            )
        go = jnp.where(depth >= wave, jnp.max(mask), 0)
        slots = renew(slots, go)
    arrived = list(slots)
    for step in far_first(senders)[:-1]:
        arrived[step] = lax.ppermute(slots[step], "trace", [(j, (j + step) % senders) for j in range(senders)])

    traces = pl.pallas_call(
        lambda *refs: write_kernel(owned, senders, stored, batches, *refs),
        out_shape=jax.ShapeDtypeStruct((batches, owned, width, shots), dtype),
        in_specs=[SMEM] + [ANY] * (senders + 1),
        out_specs=ANY,
        scratch_shapes=[
            pltpu.VMEM((senders,) + tile, dtype),
            pltpu.VMEM(tile, jnp.float32),
            pltpu.VMEM((senders,) + tile, dtype),
            pltpu.SMEM((senders,), jnp.int32),
            DMA((senders,)),
            DMA((senders, batches)),
        ],
        input_output_aliases={1 + senders: 0},
        compiler_params=PARAMS,
        name="write",
    )(table, *arrived, traces)
    return traces.reshape(1, batches, local, shots)


def solution(mesh):
    placed = (
        P("layer", "trace", None, None),
        P("layer", None, "trace", None),
        P("layer", None, None),
        P("layer", "trace", None),
    )
    return jax.shard_map(
        body, mesh=mesh, in_specs=placed, out_specs=P("layer", None, "trace", None), check_vma=False
    )
```

```python
import jax
import jax.numpy as jnp
from jax import lax
from jax.experimental import pallas as pl
from jax.experimental.pallas import tpu as pltpu
from jax.sharding import PartitionSpec as P


AXES = ("layer", "trace")
SMEM = pl.BlockSpec(memory_space=pltpu.SMEM)
ANY = pl.BlockSpec(memory_space=pl.ANY)
PARAMS = pltpu.CompilerParams(vmem_limit_bytes=67043328)
DMA = pltpu.SemaphoreType.DMA


def owner_of(row, owned):
    if owned & (owned - 1) == 0:
        return lax.shift_right_logical(row, jnp.int32(owned.bit_length() - 1))
    return lax.div(row, jnp.int32(owned))


def far_first(senders):
    return sorted(range(senders), key=lambda step: abs(2 * step - senders))


def read_table(table, senders, stored):
    held = senders * stored

    def rows(sender, block):
        return table[sender * stored + block]

    def cols(block):
        return table[held + block]

    def more(at):
        return table[held + stored + 1 + at]

    return rows, cols, table[held + stored], more


def first_kernel(senders, owned, rows_ref, cols_ref, source, blocks, *refs):
    slots, refs = refs[:senders], refs[senders:]
    operand, pieces, made, op_sem, in_sem, slot_sem = refs
    stored, _ = blocks.shape[:2]
    place = lax.axis_index("trace")
    batches, shots = source.shape[0], source.shape[-1]

    def rows(sender, block):
        return rows_ref[0, sender, block]

    def load(block):
        return pltpu.make_async_copy(blocks.at[block], operand.at[block], op_sem.at[block])

    def fetch(block, batch):
        return pltpu.make_async_copy(
            source.at[batch, cols_ref[0, 0, block] - place * owned],
            pieces.at[block, :, pl.ds(batch * shots, shots)],
            in_sem.at[block, batch],
        )

    def give(block, slot):
        return pltpu.make_async_copy(made.at[block], slots[slot], slot_sem.at[block])

    @pl.loop(0, stored)
    def _(block):
        for batch in range(batches):
            fetch(block, batch).start()
        load(block).start()

    @pl.loop(0, stored)
    def _(block):
        for batch in range(batches):
            fetch(block, batch).wait()
        load(block).wait()
        product = jnp.dot(operand[block], pieces[block], preferred_element_type=jnp.float32)
        for batch in range(batches):
            made[block, batch] = product[:, batch * shots : (batch + 1) * shots].astype(made.dtype)
        owner = owner_of(rows(place, block), owned)
        shift = lax.rem(owner - place + senders, senders)
        for slot in range(senders):

            @pl.when(shift == slot)
            def _():
                give(block, slot).start()

    @pl.loop(0, stored)
    def _(block):
        give(block, 0).wait()


def renew_kernel(senders, owned, others, table, source, blocks, *refs):
    recv, refs = refs[:senders], refs[2 * senders + others :]
    slots, refs = refs[:senders], refs[senders:]
    operand, pieces, arrived, total, made, op_sem, in_sem, recv_sem, slot_sem = refs
    stored, _ = blocks.shape[:2]
    rows, cols, place, more = read_table(table, senders, stored)
    go = more(0) > 0

    def match(block, sender):
        return more(1 + block * (senders + 1) + sender)

    batches, shots = source.shape[0], source.shape[-1]

    def load(block):
        return pltpu.make_async_copy(blocks.at[block], operand.at[block], op_sem.at[block])

    def fetch(block, batch):
        return pltpu.make_async_copy(
            source.at[batch, cols(block) - place * owned],
            pieces.at[block, :, pl.ds(batch * shots, shots)],
            in_sem.at[block, batch],
        )

    def take(step):
        return pltpu.make_async_copy(recv[step], arrived.at[step], recv_sem.at[step])

    def give(block, slot):
        return pltpu.make_async_copy(made.at[block], slots[slot], slot_sem.at[block])

    def hits(block):
        return match(block, senders)

    def sender_at(step):
        return lax.rem(place - step + senders, senders)

    @pl.when(go)
    def _():
        for step in range(senders):

            @pl.when(match(stored, sender_at(step)) > 0)
            def _():
                take(step).start()

        @pl.loop(0, stored)
        def _(block):
            @pl.when(hits(block) > 0)
            def _():
                for batch in range(batches):
                    fetch(block, batch).start()
                load(block).start()

        for step in range(senders):

            @pl.when(match(stored, sender_at(step)) > 0)
            def _():
                take(step).wait()

        @pl.loop(0, stored)
        def _(block):
            @pl.when(hits(block) > 0)
            def _():
                total[...] = jnp.zeros_like(total)

                @pl.loop(0, senders)
                def _(step):
                    @pl.when(match(block, sender_at(step)) > 0)
                    def _():
                        total[...] += arrived[step].astype(jnp.float32)

                for batch in range(batches):
                    fetch(block, batch).wait()
                for batch in range(batches):
                    lanes = pl.ds(batch * shots, shots)
                    incoming = total[batch].astype(pieces.dtype).astype(jnp.float32)
                    pieces[block, :, lanes] = (
                        incoming + pieces[block, :, lanes].astype(jnp.float32)
                    ).astype(pieces.dtype)
                load(block).wait()
                product = jnp.dot(operand[block], pieces[block], preferred_element_type=jnp.float32)
                for batch in range(batches):
                    made[block, batch] = product[:, batch * shots : (batch + 1) * shots].astype(made.dtype)
                owner = owner_of(rows(place, block), owned)
                for slot in range(senders):

                    @pl.when(lax.rem(owner - place + senders, senders) == slot)
                    def _():
                        give(block, slot).start()

        @pl.loop(0, stored)
        def _(block):
            @pl.when(hits(block) > 0)
            def _():
                give(block, 0).wait()


def hit_rows(rows, senders, place, owned, stored, here):
    first = place * owned

    @pl.loop(0, senders)
    def _(sender):
        row = jnp.int32(-1)
        for other in range(stored):
            value = rows(sender, other) - first
            row = jnp.where((value >= 0) & (value < owned), value, row)
        here[sender] = row


def zero_kernel(owned, senders, stored, batches, table, after, out, nothing, here, sem):
    rows, _, place, _ = read_table(table, senders, stored)
    hit_rows(rows, senders, place, owned, stored, here)
    nothing[...] = jnp.zeros_like(nothing)

    def free(row):
        total = jnp.int32(0)
        for sender in range(senders):
            total += (here[sender] == row).astype(jnp.int32)
        return total == 0

    def put(batch, row):
        return pltpu.make_async_copy(nothing, out.at[batch, row], sem.at[batch, row])

    @pl.loop(0, owned)
    def _(row):
        @pl.when(free(row))
        def _():
            for batch in range(batches):
                put(batch, row).start()

    @pl.loop(0, owned)
    def _(row):
        @pl.when(free(row))
        def _():
            for batch in range(batches):
                put(batch, row).wait()


def write_kernel(owned, senders, stored, batches, table, *refs):
    recv, refs = refs[:senders], refs[senders + 1 :]
    out, arrived, total, made, here, in_sem, out_sem = refs
    rows, _, place, _ = read_table(table, senders, stored)
    hit_rows(rows, senders, place, owned, stored, here)

    def take(step, sender):
        return pltpu.make_async_copy(recv[step], arrived.at[sender], in_sem.at[sender])

    def put(sender, batch, box):
        return pltpu.make_async_copy(box.at[sender, batch], out.at[batch, here[sender]], out_sem.at[sender, batch])

    def count(sender, first, last):
        total = jnp.int32(0)
        for other in range(senders):
            same = (here[other] == here[sender]) & (other >= first) & (other < last)
            total += same.astype(jnp.int32)
        return total

    for step in range(senders):
        sender = lax.rem(place - step + senders, senders)

        @pl.when(here[sender] >= 0)
        def _():
            take(step, sender).start()

    @pl.loop(0, senders)
    def _(sender):
        @pl.when((here[sender] >= 0) & (count(sender, 0, sender) == 0))
        def _():
            more = count(sender, sender + 1, senders)
            take(0, sender).wait()

            @pl.when(more == 0)
            def _():
                for batch in range(batches):
                    put(sender, batch, arrived).start()

            @pl.when(more > 0)
            def _():
                total[...] = arrived[sender].astype(jnp.float32)

                @pl.loop(sender + 1, senders)
                def _(other):
                    @pl.when(here[other] == here[sender])
                    def _():
                        take(0, other).wait()
                        total[...] += arrived[other].astype(jnp.float32)

                made[sender] = total[...].astype(made.dtype)
                for batch in range(batches):
                    put(sender, batch, made).start()

    @pl.loop(0, senders)
    def _(sender):
        @pl.when((here[sender] >= 0) & (count(sender, 0, sender) == 0))
        def _():
            for batch in range(batches):
                put(sender, batch, made).wait()


def body(operators, sources, row_block, col_block):
    place = lax.axis_index("trace")
    depth = lax.axis_index("layer")
    senders = lax.axis_size("trace")
    layers = lax.axis_size("layer")
    blocks = operators[0]
    rows = row_block[0]
    stored, width = blocks.shape[0], blocks.shape[-1]
    batches, local, shots = sources.shape[1:]
    owned = local // width
    source = sources.reshape(batches, owned, width, shots)
    cols = col_block[0, 0]
    table = jnp.concatenate([rows.reshape(-1), cols, place[None].astype(jnp.int32)])
    dtype = sources.dtype
    tile = (batches, width, shots)
    slot = jax.ShapeDtypeStruct(tile, dtype)

    def pairs(step, top=0):
        return [
            (i * senders + j, (i + 1) * senders + (j + step) % senders)
            for i in range(top, layers - 1)
            for j in range(senders)
        ]

    slots = pl.pallas_call(
        lambda *refs: first_kernel(senders, owned, *refs),
        out_shape=(slot,) * senders,
        in_specs=[SMEM] * 2 + [ANY] * 2,
        out_specs=(ANY,) * senders,
        scratch_shapes=[
            pltpu.VMEM((stored, width, width), dtype),
            pltpu.VMEM((stored, width, batches * shots), dtype),
            pltpu.VMEM((stored,) + tile, dtype),
            DMA((stored,)),
            DMA((stored, batches)),
            DMA((stored,)),
        ],
        compiler_params=PARAMS,
        name="first",
    )(row_block, col_block, source, blocks)
    recv = [None] * senders
    for step in far_first(senders):
        recv[step] = lax.ppermute(slots[step], AXES, pairs(step))

    total = layers * senders
    mine, slots = lax.optimization_barrier((table, slots))
    mine = jnp.broadcast_to(mine[None], (total, mine.shape[0]))
    known = lax.all_to_all(mine, AXES, split_axis=0, concat_axis=0, tiled=True)
    known = known.reshape(layers, senders, -1)
    blocks_all = senders * stored
    rows_all = known[:, 0, :blocks_all]
    cols_all = known[:, :, blocks_all : blocks_all + stored].reshape(layers, blocks_all)
    feeds = rows_all[:-1, :, None] == cols_all[1:, None, :]
    read = jnp.any(feeds, axis=2)
    home = jnp.repeat(jnp.arange(senders, dtype=jnp.int32), stored)
    shift = (rows_all[:-1] // owned - home[None, :]) % senders
    steps = jnp.arange(senders, dtype=jnp.int32)
    changed = jnp.any(feeds, axis=1)
    masks = []
    for wave in range(2, layers):
        below = jnp.concatenate([jnp.zeros((1, blocks_all), bool), changed[:-1]])
        again = below & read
        mask = jnp.any(again[:, :, None] & (shift[:, :, None] == steps), axis=(0, 1)).astype(jnp.int32)
        masks.append(mask)
        changed = jnp.any(feeds & below[:, :, None], axis=1)

    above = lax.dynamic_index_in_dim(rows_all, jnp.maximum(depth - 1, 0), 0, keepdims=False)
    above = above.reshape(senders, stored)
    match = jnp.any((above[None] == cols[:, None, None]) & (depth > 0), axis=2).astype(jnp.int32)
    match = jnp.concatenate([match, jnp.max(match, axis=0, keepdims=True)])
    match = jnp.concatenate([match, jnp.max(match, axis=1, keepdims=True)], axis=1)

    def renew(slots, go, after=()):
        return pl.pallas_call(
            lambda *refs: renew_kernel(senders, owned, len(after), *refs),
            out_shape=(slot,) * senders,
            in_specs=[SMEM] + [ANY] * (2 + 2 * senders + len(after)),
            out_specs=(ANY,) * senders,
            scratch_shapes=[
                pltpu.VMEM((stored, width, width), dtype),
                pltpu.VMEM((stored, width, batches * shots), dtype),
                pltpu.VMEM((senders,) + tile, dtype),
                pltpu.VMEM(tile, jnp.float32),
                pltpu.VMEM((stored,) + tile, dtype),
                DMA((stored,)),
                DMA((stored, batches)),
                DMA((senders,)),
                DMA((stored,)),
            ],
            input_output_aliases={3 + senders + at: at for at in range(senders)},
            compiler_params=PARAMS,
            name="renew",
        )(jnp.concatenate([table, go[None], match.reshape(-1)]), source, blocks, *recv, *slots, *after)

    traces = pl.pallas_call(
        lambda *refs: zero_kernel(owned, senders, stored, batches, *refs),
        out_shape=jax.ShapeDtypeStruct((batches, owned, width, shots), dtype),
        in_specs=[SMEM, ANY],
        out_specs=ANY,
        scratch_shapes=[pltpu.VMEM((width, shots), dtype), pltpu.SMEM((senders,), jnp.int32), DMA((batches, owned))],
        compiler_params=PARAMS,
        name="zeros",
    )(table, mine)

    slots = renew(slots, jnp.int32(1), (traces,))
    for wave, mask in enumerate(masks, 2):
        group = 4 if wave == 2 and senders <= 8 else 2
        for low in range(0, senders, group):
            near = range(low, min(low + group, senders))

            def resend(which):
                return lambda new, old: tuple(
                    lax.ppermute(new[at], AXES, pairs(step, wave - 1)) if which >> at & 1 else old[at]
                    for at, step in enumerate(near)
                )

            code = sum(mask[step] << at for at, step in enumerate(near))
            recv[low : low + group] = lax.switch(
                code,
                [resend(which) for which in range(1 << len(near))],
                tuple(slots[low : low + group]),
                tuple(recv[low : low + group]),
            )
        go = jnp.where(depth >= wave, jnp.max(mask), 0)
        slots = renew(slots, go)
    arrived = list(slots)
    for step in far_first(senders)[:-1]:
        arrived[step] = lax.ppermute(slots[step], "trace", [(j, (j + step) % senders) for j in range(senders)])

    traces = pl.pallas_call(
        lambda *refs: write_kernel(owned, senders, stored, batches, *refs),
        out_shape=jax.ShapeDtypeStruct((batches, owned, width, shots), dtype),
        in_specs=[SMEM] + [ANY] * (senders + 1),
        out_specs=ANY,
        scratch_shapes=[
            pltpu.VMEM((senders,) + tile, dtype),
            pltpu.VMEM(tile, jnp.float32),
            pltpu.VMEM((senders,) + tile, dtype),
            pltpu.SMEM((senders,), jnp.int32),
            DMA((senders,)),
            DMA((senders, batches)),
        ],
        input_output_aliases={1 + senders: 0},
        compiler_params=PARAMS,
        name="write",
    )(table, *arrived, traces)
    return traces.reshape(1, batches, local, shots)


def solution(mesh):
    placed = (
        P("layer", "trace", None, None),
        P("layer", None, "trace", None),
        P("layer", None, None),
        P("layer", "trace", None),
    )
    return jax.shard_map(
        body, mesh=mesh, in_specs=placed, out_specs=P("layer", None, "trace", None), check_vma=False
    )
```
